256 devices in a mesh: dp: 8 (over x, core), seq: 32 (over y, z).
Axes of the slice: x: 4, y: 4, z: 8, core: 2. Of those that a mesh axis runs over, the one named last changes fastest.
Arguments:
- tokens: bfloat16 [8, 16384, 1024], P('dp', 'seq'), may hold values from -6 to 6
- cotangent: bfloat16 [8, 16384, 1024], P('dp', 'seq'), may hold values from -6 to 6
- gain_mix: float32 [1024], replicated, may hold values from 0.25 to 1.75
- gain_mlp: float32 [1024], replicated, may hold values from 0.25 to 1.75
- fine_factor: bfloat16 [8, 128, 128], replicated, may hold values from -3.2 to 3.2, as said below
- coarse_factor: bfloat16 [8, 128, 128], replicated, may hold values from -3.2 to 3.2, as said below
- w_gate_up: bfloat16 [1024, 2048], P(('dp', 'seq')), may hold values from -0.1875 to 0.1875
- w_down: bfloat16 [1024, 1024], P(('dp', 'seq')), may hold values from -0.1875 to 0.1875
Outputs:
- layer_out: bfloat16 [8, 16384, 1024], P('dp', 'seq')
- grad_input: bfloat16 [8, 16384, 1024], P('dp', 'seq')
- grad_gate_up: float32 [1024, 2048], P(('dp', 'seq'))
- grad_down: float32 [1024, 1024], P(('dp', 'seq'))
- grad_fine: float32 [8, 128, 128], replicated
- grad_coarse: float32 [8, 128, 128], replicated
- grad_gain_mix: float32 [1024], replicated
- grad_gain_mlp: float32 [1024], replicated
The draws below stay inside these ranges and needn't reach their ends.
Inputs may be any that keep to these rules, and one draw needn't show every extreme that they name: `fine_factor`: each group's factor is lower triangular: entries above the diagonal are zero. `coarse_factor`: each group's factor is lower triangular: entries above the diagonal are zero.
All inputs are finite; a program needn't handle non-finite values.
Results may differ from the reference program's by a relative error of at most 0.012.
Values may be sent and summed in bfloat16 or wider, within the bound.
A program may use at most 128 MiB of HBM per device.

```python
import math
import jax
import jax.numpy as jnp
from jax import lax

D = 1024
FF = 1024
NB = 128
NC = 128
GW = 128
G = 8
LEN = 16384
SEQS = 8


def factor_draw(key, groups, order):
    entries_raw = jnp.clip(jax.random.normal(key, (groups, order, order), jnp.float32), -4.0, 4.0)
    row_index = lax.broadcasted_iota(jnp.int32, (groups, order, order), 1)
    col_index = lax.broadcasted_iota(jnp.int32, (groups, order, order), 2)
    lower_part = 0.8 * entries_raw * lax.rsqrt(row_index.astype(jnp.float32) + 1.0)
    diagonal_part = 1.0 + 0.2 * jnp.tanh(entries_raw)
    factor_values = jnp.where(col_index < row_index, lower_part, jnp.where(col_index == row_index, diagonal_part, 0.0))
    return factor_values.astype(jnp.bfloat16)


def draw_fine_factor(key, part):
    return factor_draw(jax.random.fold_in(key, 3), G, NB)


def draw_coarse_factor(key, part):
    return factor_draw(jax.random.fold_in(key, 7), G, NC)


def spiked(array, rng, source, target, shards_of, factor):
    owner, partner = [(jnp.arange(array.shape[dim]) // (array.shape[dim] // shards_of)).reshape([-1 if axis == dim else 1 for axis in range(array.ndim)]) for dim in (source, target)]
    chosen = jax.random.permutation(rng, shards_of)[partner]
    strong = (owner == chosen) | (owner == (partner + shards_of // 2) % shards_of)
    return jnp.where(strong, factor * array, array)


def levels(own_key, shape, cuts, low, high):
    def one(axis_at, shards_of):
        draws = jax.random.uniform(jax.random.fold_in(jax.random.fold_in(own_key, 6), axis_at), (shards_of,), jnp.float32, low / len(cuts), high / len(cuts))
        return jnp.repeat(jnp.exp(draws), shape[axis_at] // shards_of).reshape((-1,) + (1,) * (len(shape) - axis_at - 1))

    loudness = one(*cuts[0])
    for cut in cuts[1:]:
        loudness = loudness * one(*cut)
    return loudness


def scatter_about(rng, extent, spread, bound, split=(), kind=jnp.bfloat16):
    loudness = levels(rng, extent, split, -0.22, 0.18) if split else 1.0
    values = jax.random.normal(rng, extent, jnp.float32) * spread * loudness
    return jnp.minimum(jnp.maximum(values, -bound), bound).astype(kind)


def heavy_noise(stream_key, extent, deviation, most, pieces, heavy, held_as=jnp.bfloat16):
    result = deviation * jax.random.normal(stream_key, extent, jnp.float32)
    if pieces:
        result = result * levels(stream_key, extent, pieces, -0.22, 0.18)
    return jnp.clip(spiked(result, jax.random.fold_in(stream_key, 3), *heavy), -most, most).astype(held_as)


def setup_inputs(seed: int = 0) -> dict:
    splits = jax.random.split(jax.random.key(seed), 9)
    tokens = heavy_noise(splits[0], (SEQS, LEN, D), 1.0, 6.0, ((0, 8), (1, 32)), (1, 2, 32, 2.75))
    cotangent = scatter_about(splits[1], (SEQS, LEN, D), 1.0, 6.0, ((0, 8), (1, 32)))
    gain_mix = jnp.clip(1.0 + 0.15 * jax.random.normal(splits[2], (D,), jnp.float32), 0.25, 1.75)
    gain_mlp = jnp.clip(1.0 + 0.15 * jax.random.normal(splits[3], (D,), jnp.float32), 0.25, 1.75)
    fine_factor = draw_fine_factor(jax.random.fold_in(splits[8], 71), 0)
    coarse_factor = draw_coarse_factor(jax.random.fold_in(splits[8], 71), 0)
    w_gate_up = scatter_about(splits[6], (D, 2 * FF), D ** -0.5, 0.1875, ((0, 256),))
    w_down = scatter_about(splits[7], (D, FF), FF ** -0.5, 0.1875, ((0, 256),))
    return {"tokens": tokens, "cotangent": cotangent, "gain_mix": gain_mix, "gain_mlp": gain_mlp, "fine_factor": fine_factor, "coarse_factor": coarse_factor, "w_gate_up": w_gate_up, "w_down": w_down}


epsilon = 1e-05

def widen(values):
    return lax.optimization_barrier(values.astype(jnp.bfloat16)).astype(jnp.float32)

def norm_rows(values):
    scale_inv = lax.rsqrt(lax.optimization_barrier(jnp.mean(values * values, axis=-1, keepdims=True)) + epsilon)
    return (values * scale_inv, scale_inv)

def norm_back(upstream, normed, scale_inv):
    return scale_inv * (upstream - normed * lax.optimization_barrier(jnp.mean(upstream * normed, axis=-1, keepdims=True)))

def silu_parts(gate_pre):
    squash = jax.nn.sigmoid(gate_pre)
    return (gate_pre * squash, squash * (1.0 + gate_pre * (1.0 - squash)))

def reference(tokens, cotangent, gain_mix, gain_mlp, fine_factor, coarse_factor, w_gate_up, w_down):
    fine_weights = fine_factor.astype(jnp.float32)
    coarse_weights = coarse_factor.astype(jnp.float32)

    def one_sequence(totals, sequence_pair):
        inputs, upstream_out = sequence_pair
        source = inputs.astype(jnp.float32)
        normed_mix, inv_mix = norm_rows(source)
        gated_in = widen(normed_mix * gain_mix)
        blocked = gated_in.reshape(NC, NB, G, GW)
        fine_mixed = widen(jnp.einsum('gpq,aqgc->apgc', fine_weights, blocked))
        coarse_mixed = widen(jnp.einsum('gpq,qbgc->pbgc', coarse_weights, fine_mixed))
        mixed = coarse_mixed.reshape(LEN, D)
        after_mix = source + mixed * gated_in
        normed_mlp, inv_mlp = norm_rows(after_mix)
        mlp_in = (normed_mlp * gain_mlp).astype(jnp.bfloat16)
        both = jnp.dot(mlp_in, w_gate_up, preferred_element_type=jnp.float32)
        gate_pre = both[:, :FF]
        upward = both[:, FF:]
        silu_gate, silu_slope = silu_parts(gate_pre)
        activation = (silu_gate * upward).astype(jnp.bfloat16)
        layer = (after_mix + jnp.dot(activation, w_down.T, preferred_element_type=jnp.float32)).astype(jnp.bfloat16)
        upstream = upstream_out.astype(jnp.float32)
        back_act = widen(jnp.dot(upstream_out, w_down, preferred_element_type=jnp.float32))
        back_both = jnp.concatenate([back_act * upward * silu_slope, back_act * silu_gate], axis=1).astype(jnp.bfloat16)
        back_mlp_in = jnp.dot(back_both, w_gate_up.T, preferred_element_type=jnp.float32)
        gain_mlp_term = lax.optimization_barrier(jnp.sum(back_mlp_in * normed_mlp, axis=0))
        back_after = upstream + norm_back(back_mlp_in * gain_mlp, normed_mlp, inv_mlp)
        back_mixed = widen(back_after * gated_in).reshape(NC, NB, G, GW)
        back_fine = widen(jnp.einsum('gpq,pbgc->qbgc', coarse_weights, back_mixed))
        coarse_term = jnp.einsum('pbgc,qbgc->gpq', back_mixed, fine_mixed)
        back_blocked = jnp.einsum('gpq,apgc->aqgc', fine_weights, back_fine).reshape(LEN, D)
        fine_term = jnp.einsum('apgc,aqgc->gpq', back_fine, blocked)
        back_hidden = back_after * mixed + back_blocked
        gain_mix_term = lax.optimization_barrier(jnp.sum(back_hidden * normed_mix, axis=0))
        grad_in = (back_after + norm_back(back_hidden * gain_mix, normed_mix, inv_mix)).astype(jnp.bfloat16)
        gate_up_term = jnp.dot(mlp_in.T, back_both, preferred_element_type=jnp.float32)
        down_term = jnp.dot(upstream_out.T, activation, preferred_element_type=jnp.float32)
        new_totals = (totals[0] + gate_up_term, totals[1] + down_term, totals[2] + fine_term, totals[3] + coarse_term, totals[4] + gain_mix_term, totals[5] + gain_mlp_term)
        return (new_totals, (layer, grad_in))
    start_totals = (jnp.zeros((D, 2 * FF), jnp.float32), jnp.zeros((D, FF), jnp.float32), jnp.zeros((G, NB, NB), jnp.float32), jnp.zeros((G, NC, NC), jnp.float32), jnp.zeros((D,), jnp.float32), jnp.zeros((D,), jnp.float32))
    final_totals, stacked = lax.scan(one_sequence, start_totals, (tokens, cotangent))
    scale_tokens = 1.0 / math.sqrt(SEQS * LEN)
    grad_fine = jnp.tril(final_totals[2]) * (1.0 / math.sqrt(SEQS * NC * GW))
    grad_coarse = jnp.tril(final_totals[3]) * (1.0 / math.sqrt(SEQS * NB * GW))
    return (stacked[0], stacked[1], final_totals[0] * scale_tokens, final_totals[1] * scale_tokens, grad_fine, grad_coarse, final_totals[4] * scale_tokens, final_totals[5] * scale_tokens)
```

```python
import math

import jax
import jax.numpy as jnp
from jax import lax
from jax.experimental import pallas as pl
from jax.experimental.pallas import tpu as pltpu
from jax.sharding import PartitionSpec as P

D = 1024
FF = 1024
NB = 128
NC = 128
GW = 128
G = 8
NX, NY, NZ = 4, 4, 8
BL = 4
QW = 256
BW = 16
ROWS = BL * NB
WC = 3 * FF
EPS = 1e-05
MESH = pl.DeviceIdType.MESH
F32 = jnp.float32
BF16 = jnp.bfloat16


def place():
    dp = lax.axis_index("dp")
    seq = lax.axis_index("seq")
    return dp // 2, dp % 2, seq // NZ, seq % NZ


def send(src, dst, ssem, rsem, dp, seq):
    return pltpu.make_async_remote_copy(
        src_ref=src,
        dst_ref=dst,
        send_sem=ssem,
        recv_sem=rsem,
        device_id=(dp, seq),
        device_id_type=MESH,
    )


def greet(x, c, y, z):
    bar = pltpu.get_barrier_semaphore()

    def one(dp, seq):
        pl.semaphore_signal(bar, inc=1, device_id=(dp, seq), device_id_type=MESH)

    def plane(k, carry):
        one(2 * x + c, ((y + k // NZ) % NY) * NZ + (z + k % NZ) % NZ)
        return carry

    lax.fori_loop(1, NY * NZ, plane, 0)
    for k in range(1, NX):
        one(2 * ((x + k) % NX) + c, y * NZ + z)
    one(2 * x + 1 - c, y * NZ + z)
    return bar, NY * NZ - 1 + NX - 1 + 1


def dot(a, b, ca=1, cb=0):
    return lax.dot_general(a, b, (((ca,), (cb,)), ((), ())), preferred_element_type=F32)


def exchange_in(src, dst, ssem, rsem, x, c, y, z):
    me = y * NZ + z

    def copy(k):
        ty = (y + k // NZ) % NY
        tz = (z + k % NZ) % NZ
        return send(
            src.at[:, pl.ds(pl.multiple_of(BW * tz, BW), BW), pl.ds(pl.multiple_of(QW * ty, QW), QW)],
            dst.at[pl.ds(BL * me, BL)],
            ssem.at[k],
            rsem.at[k],
            2 * x + c,
            ty * NZ + tz,
        )

    return copy


def exchange_out(src, dst, ssem, rsem, x, c, y, z):
    def copy(k):
        ty = (y + k // NZ) % NY
        tz = (z + k % NZ) % NZ
        to = ty * NZ + tz
        return send(
            src.at[pl.ds(BL * to, BL)],
            dst.at[:, pl.ds(pl.multiple_of(BW * z, BW), BW), pl.ds(pl.multiple_of(QW * y, QW), QW)],
            ssem.at[k],
            rsem.at[k],
            2 * x + c,
            to,
        )

    return copy


def start_all(copy, n):
    def body(k, carry):
        copy(k).start()
        return carry

    lax.fori_loop(1, n, body, 0)


def recv_all(copy, n):
    def body(k, carry):
        copy(k).wait_recv()
        return carry

    lax.fori_loop(1, n, body, 0)


def sent_all(copy, n):
    def body(k, carry):
        copy(k).wait_send()
        return carry

    lax.fori_loop(1, n, body, 0)


def to_rows(src, tall):
    def body(i, carry):
        v = src[pl.ds(8 * i, 8)].reshape(8 * BW, QW).astype(F32)
        at = pl.ds(pl.multiple_of(8 * BW * i, 8 * BW), 8 * BW)
        tall[0, at, :] = v[:, :GW]
        tall[1, at, :] = v[:, GW:]
        return carry

    lax.fori_loop(0, NC // 8, body, 0)


def from_rows(tall, dst):
    def body(i, carry):
        at = pl.ds(pl.multiple_of(8 * BW * i, 8 * BW), 8 * BW)
        v = jnp.concatenate([tall[0, at, :], tall[1, at, :]], axis=1).astype(BF16)
        dst[pl.ds(8 * i, 8)] = v.reshape(8, BW, QW)
        return carry

    lax.fori_loop(0, NC // 8, body, 0)


def own_in(src, dst, x, c, y, z):
    me = y * NZ + z
    dst[pl.ds(BL * me, BL)] = src[
        :, pl.ds(pl.multiple_of(BW * z, BW), BW), pl.ds(pl.multiple_of(QW * y, QW), QW)
    ]


def own_out(src, dst, x, c, y, z):
    me = y * NZ + z
    dst[:, pl.ds(pl.multiple_of(BW * z, BW), BW), pl.ds(pl.multiple_of(QW * y, QW), QW)] = src[
        pl.ds(BL * me, BL)
    ]


def forward_kernel(
    tok, gain, fine, coarse, wgu, wdn,
    mixed, hid, moved, fgu, fdn,
    fm, back, tall, tall2, wz, wrow,
    s_in, r_in, s_out, r_out, s_z, r_z, s_y, r_y, s_x, r_x, s_c, r_c,
):
    x, c, y, z = place()
    dp = 2 * x + c
    seq = y * NZ + z
    bar, count = greet(x, c, y, z)

    wz[pl.ds(z, 1), :, : 2 * FF] = wgu[...].reshape(1, 4, 2 * FF)
    wz[pl.ds(z, 1), :, 2 * FF :] = wdn[...].reshape(1, 4, FF)

    def norm(i, carry):
        a = i // 4
        at = pl.ds(pl.multiple_of((i % 4) * 32, 32), 32)
        v = tok[a, at, :].astype(F32)
        inv = lax.rsqrt(jnp.mean(v * v, axis=-1, keepdims=True) + EPS)
        hid[a, at, :] = ((v * inv) * gain[...]).astype(BF16)
        return carry

    lax.fori_loop(0, BL * 4, norm, 0)

    pl.semaphore_wait(bar, count)

    def z_copy(k):
        tz = (z + k) % NZ
        return send(wz.at[z], wz.at[z], s_z.at[k], r_z.at[k], dp, y * NZ + tz)

    start_all(z_copy, NZ)

    for g in range(G):
        cols = slice(g * GW, (g + 1) * GW)
        for a in range(BL):
            fm[a, :, cols] = dot(fine[g], hid[a, :, cols]).astype(BF16)

    c_in = exchange_in(fm, moved, s_in, r_in, x, c, y, z)
    start_all(c_in, NY * NZ)
    own_in(fm, moved, x, c, y, z)

    recv_all(z_copy, NZ)
    for zz in range(NZ):
        wrow[4 * zz : 4 * zz + 4, :] = wz[zz].astype(F32)
    my = pl.ds(pl.multiple_of(dp * 128 + y * 32, 32), 32)
    fgu[my, :] = wrow[:, : 2 * FF].astype(BF16)
    fdn[my, :] = wrow[:, 2 * FF :].astype(BF16)

    def pair(k, at, ss, rs, tdp, tseq):
        return (
            send(fgu.at[at, :], fgu.at[at, :], ss.at[0, k], rs.at[0, k], tdp, tseq),
            send(fdn.at[at, :], fdn.at[at, :], ss.at[1, k], rs.at[1, k], tdp, tseq),
        )

    y_copies = [pair(k, my, s_y, r_y, dp, ((y + k) % NY) * NZ + z) for k in range(1, NY)]
    for two in y_copies:
        for one in two:
            one.start()
    for two in y_copies:
        for one in two:
            one.wait_recv()

    my_x = pl.ds(pl.multiple_of(dp * 128, 128), 128)
    x_copies = [pair(k, my_x, s_x, r_x, 2 * ((x + k) % NX) + c, seq) for k in range(1, NX)]
    for two in x_copies:
        for one in two:
            one.start()

    def core_copy(k):
        at = pl.ds(pl.multiple_of((2 * ((x + NX - k) % NX) + c) * 128, 128), 128)
        return pair(k, at, s_c, r_c, 2 * x + 1 - c, seq)

    for one in core_copy(0):
        one.start()

    recv_all(c_in, NY * NZ)
    to_rows(moved, tall)
    for b in range(BW):
        for h in range(2):
            v = tall[h, pl.ds(b, NC, stride=BW), :].astype(BF16)
            tall2[h, pl.ds(b, NC, stride=BW), :] = dot(coarse[2 * y + h], v)
    from_rows(tall2, back)
    c_out = exchange_out(back, mixed, s_out, r_out, x, c, y, z)
    start_all(c_out, NY * NZ)
    own_out(back, mixed, x, c, y, z)

    for k in range(1, NX):
        for one in x_copies[k - 1]:
            one.wait_recv()
        for one in core_copy(k):
            one.start()
    recv_all(c_out, NY * NZ)
    for k in range(NX):
        for one in core_copy(k):
            one.wait_recv()
            one.wait_send()
    for two in y_copies + x_copies:
        for one in two:
            one.wait_send()
    sent_all(z_copy, NZ)
    sent_all(c_in, NY * NZ)
    sent_all(c_out, NY * NZ)


def backward_kernel(
    bm, moved, fine, coarse, mlp_in, bboth, cot, act, bafter, mixed, hid, tok, gain, glm,
    gin, ogu, odn, ofine, ocoarse, ogain,
    xin, xout, bfine, bhid, tall, tall2, tallm,
    pbuf, crecv, xrecv, acc, ysend, yrecv, zbuf, zrecv,
    v32, v16, vc, vxs, vx, v2, vys, vy, vz, vzr, az, v3, ay, every,
    gc, gx, gy, gz,
    s_in, r_in, s_out, r_out, s_c, r_c, s_x, r_x, s_y, r_y, s_z, r_z,
    ts, tr, gs, gr,
):
    x, c, y, z = place()
    dp = 2 * x + c
    seq = y * NZ + z
    sib = 2 * x + 1 - c
    bar, count = greet(x, c, y, z)
    pl.semaphore_wait(bar, count)

    c_in = exchange_in(bm, xin, s_in, r_in, x, c, y, z)
    start_all(c_in, NY * NZ)
    own_in(bm, xin, x, c, y, z)

    def part(d, put):
        at = pl.ds(pl.multiple_of(d * 128, 128), 128)
        lhs = mlp_in[:, at]
        for n in range(4):
            cols = slice(512 * n, 512 * n + 512)
            put(cols, dot(lhs, bboth[:, cols], 0, 0))
        lhs = cot[:, at]
        for n in range(2):
            cols = slice(512 * n, 512 * n + 512)
            put(slice(2 * FF + 512 * n, 2 * FF + 512 * n + 512), dot(lhs, act[:, cols], 0, 0))

    def core_copy(k):
        d = 2 * ((x + k) % NX) + 1 - c
        return send(pbuf.at[d], crecv.at[k], s_c.at[k], r_c.at[k], sib, seq)

    def x_copy(k):
        xx = (x + k) % NX
        return send(pbuf.at[2 * xx + c], xrecv.at[k - 1], s_x.at[k], r_x.at[k], 2 * xx + c, seq)

    def first(i, carry):
        k = (i + 1) % NX
        d = 2 * ((x + k) % NX) + 1 - c

        def put(cols, v):
            pbuf[d, :, cols] = v.astype(BF16)

        part(d, put)
        core_copy(k).start()
        return carry

    lax.fori_loop(0, NX, first, 0)

    def second(k, carry):
        d = 2 * ((x + k) % NX) + c
        core_copy(k).wait_recv()

        def put(cols, v):
            pbuf[d, :, cols] = (v + crecv[k, :, cols].astype(F32)).astype(BF16)

        part(d, put)
        x_copy(k).start()
        return carry

    lax.fori_loop(1, NX, second, 0)
    core_copy(0).wait_recv()

    def put_own(cols, v):
        acc[:, cols] = v + crecv[0, :, cols].astype(F32)

    part(dp, put_own)

    recv_all(c_in, NY * NZ)
    to_rows(xin, tall)
    for b in range(BW):
        for h in range(2):
            v = tall[h, pl.ds(b, NC, stride=BW), :].astype(BF16)
            tall2[h, pl.ds(b, NC, stride=BW), :] = dot(coarse[2 * y + h], v, 0, 0)
    from_rows(tall2, xout)
    c_out = exchange_out(xout, bfine, s_out, r_out, x, c, y, z)
    start_all(c_out, NY * NZ)
    own_out(xout, bfine, x, c, y, z)

    to_rows(moved, tallm)
    for d in range(G):
        v32[d % 2, d // 2, :, GW:] = jnp.zeros((128, GW), F32)
    for h in range(2):
        total = jnp.zeros((NC, NC), F32)
        for b in range(BW):
            at = pl.ds(b, NC, stride=BW)
            total = total + dot(tall[h, at, :].astype(BF16), tallm[h, at, :].astype(BF16), 1, 1)
        v32[h, y, :, GW:] = total

    for k in range(1, NX):
        x_copy(k).wait_recv()

    def add_x(i, carry):
        at = pl.ds(pl.multiple_of(i * 16, 16), 16)
        v = acc[at, :]
        for k in range(NX - 1):
            v = v + xrecv[k, at, :].astype(F32)
        acc[at, :] = v
        return carry

    lax.fori_loop(0, 8, add_x, 0)

    def y_copy(k):
        yy = (y + k) % NY
        return send(ysend.at[yy], yrecv.at[k - 1], s_y.at[k], r_y.at[k], dp, yy * NZ + z)

    for yy in range(NY):
        ysend[yy] = acc[32 * yy : 32 * yy + 32, :].astype(BF16)
    start_all(y_copy, NY)
    recv_all(y_copy, NY)
    for part_row in range(4):
        at = pl.ds(pl.multiple_of(32 * y + 8 * part_row, 8), 8)
        v = acc[at, :]
        for k in range(NY - 1):
            v = v + yrecv[k, 8 * part_row : 8 * part_row + 8, :].astype(F32)
        zbuf[2 * part_row] = v[:4]
        zbuf[2 * part_row + 1] = v[4:]

    def z_copy(k):
        zz = (z + k) % NZ
        return send(zbuf.at[zz], zrecv.at[k - 1], s_z.at[k], r_z.at[k], dp, y * NZ + zz)

    start_all(z_copy, NZ)

    recv_all(c_out, NY * NZ)
    for g in range(G):
        cols = slice(g * GW, (g + 1) * GW)
        total = jnp.zeros((NB, NB), F32)
        for a in range(BL):
            v = bfine[a, :, cols]
            total = total + dot(v, hid[a, :, cols], 1, 1)
            bhid[a, :, cols] = bafter[a, :, cols] * mixed[a, :, cols].astype(F32) + dot(
                fine[g], v, 0, 0
            )
        v32[g % 2, g // 2, :, :GW] = total

    def last(i, total):
        a = i // 8
        at = pl.ds(pl.multiple_of((i % 8) * 16, 16), 16)
        v = tok[a, at, :].astype(F32)
        inv = lax.rsqrt(jnp.mean(v * v, axis=-1, keepdims=True) + EPS)
        normed = v * inv
        bh = bhid[a, at, :]
        w1 = bh * gain[...]
        prod = bh * normed
        center = jnp.mean(prod * gain[...], axis=-1, keepdims=True)
        gin[a, at, :] = (bafter[a, at, :] + inv * (w1 - normed * center)).astype(BF16)
        return total + prod[:8] + prod[8:]

    gm = lax.fori_loop(0, BL * 8, last, jnp.zeros((8, D), F32))
    gm = jnp.sum(gm, axis=0, keepdims=True)

    def c_small():
        return send(v16, vc, ts.at[0, 0], tr.at[0, 0], sib, seq)

    def c_gain():
        return send(gc.at[c], gc.at[c], gs.at[0, 0], gr.at[0, 0], sib, seq)

    for d in range(G):
        gc[pl.ds(c, 1), d : d + 1, :GW] = gm[:, d * GW : (d + 1) * GW].reshape(1, 1, GW)
    gc[pl.ds(c, 1), :, GW:] = glm[...].reshape(1, 8, GW)
    c_gain().start()
    v16[...] = v32[1 - c].astype(BF16)
    c_small().start()

    recv_all(z_copy, NZ)
    scale = 1.0 / math.sqrt(8 * NC * NB)
    v = zbuf[z]
    for k in range(NZ - 1):
        v = v + zrecv[k]
    v = v * scale
    ogu[...] = v[:, : 2 * FF]
    odn[...] = v[:, 2 * FF :]

    def x_small(k):
        xx = (x + k) % NX
        return send(vxs.at[xx], vx.at[k - 1], ts.at[1, k], tr.at[1, k], 2 * xx + c, seq)

    def x_gain(k):
        xx = (x + k) % NX
        return send(gx.at[x], gx.at[x], gs.at[1, k], gr.at[1, k], 2 * xx + c, seq)

    def y_small(k):
        yy = (y + k) % NY
        return send(vys.at[yy], vy.at[k - 1], ts.at[2, k], tr.at[2, k], dp, yy * NZ + z)

    def y_gain(k):
        yy = (y + k) % NY
        return send(gy.at[y], gy.at[y], gs.at[2, k], gr.at[2, k], dp, yy * NZ + z)

    def z_small(k):
        zz = (z + k) % NZ
        return send(vz.at[zz], vzr.at[k - 1], ts.at[3, k], tr.at[3, k], dp, y * NZ + zz)

    def z_gain(k):
        zz = (z + k) % NZ
        return send(gz.at[z], gz.at[z], gs.at[3, k], gr.at[3, k], dp, y * NZ + zz)

    c_gain().wait_recv()
    gx[x] = gc[0] + gc[1]
    start_all(x_gain, NX)
    c_small().wait_recv()
    for xx in range(NX):
        vxs[xx] = (v32[c, xx] + vc[xx].astype(F32)).astype(BF16)
    start_all(x_small, NX)
    v2[...] = v32[c, x] + vc[x].astype(F32)

    recv_all(x_gain, NX)
    gy[y] = (gx[0] + gx[1]) + (gx[2] + gx[3])
    start_all(y_gain, NY)
    recv_all(x_small, NX)
    v = v2[...]
    for k in range(NX - 1):
        v = v + vx[k].astype(F32)
    v2[...] = v
    for yy in range(NY):
        vys[yy] = v[32 * yy : 32 * yy + 32].astype(BF16)
    start_all(y_small, NY)

    recv_all(y_gain, NY)
    gz[z] = (gy[0] + gy[1]) + (gy[2] + gy[3])
    start_all(z_gain, NZ)
    recv_all(y_small, NY)
    v = v2[pl.ds(pl.multiple_of(32 * y, 32), 32), :]
    for k in range(NY - 1):
        v = v + vy[k].astype(F32)
    for zz in range(NZ):
        vz[zz] = v[4 * zz : 4 * zz + 4]
    start_all(z_small, NZ)
    recv_all(z_small, NZ)
    v = vz[z]
    for k in range(NZ - 1):
        v = v + vzr[k]
    az[z] = v

    def z_back(k):
        zz = (z + k) % NZ
        return send(az.at[z], az.at[z], ts.at[4, k], tr.at[4, k], dp, y * NZ + zz)

    def y_back(k):
        yy = (y + k) % NY
        return send(ay.at[y], ay.at[y], ts.at[5, k], tr.at[5, k], dp, yy * NZ + z)

    def x_back(k):
        xx = (x + k) % NX
        return send(every.at[c, x], every.at[c, x], ts.at[6, k], tr.at[6, k], 2 * xx + c, seq)

    def c_back(k):
        xx = (x + NX - k) % NX
        return send(every.at[c, xx], every.at[c, xx], ts.at[7, k], tr.at[7, k], sib, seq)

    start_all(z_back, NZ)
    recv_all(z_gain, NZ)
    v = gz[0]
    for zz in range(1, NZ):
        v = v + gz[zz]
    ogain[...] = v * scale
    recv_all(z_back, NZ)
    for zz in range(NZ):
        v3[4 * zz : 4 * zz + 4, :] = az[zz]
    ay[y] = v3[...].astype(BF16)
    start_all(y_back, NY)
    recv_all(y_back, NY)
    for yy in range(NY):
        every[c, x, 32 * yy : 32 * yy + 32, :] = ay[yy]
    start_all(x_back, NX)
    c_back(0).start()
    for k in range(1, NX):
        x_back(k).wait_recv()
        c_back(k).start()
    for k in range(NX):
        c_back(k).wait_recv()
    lower = lax.broadcasted_iota(jnp.int32, (128, 128), 0) >= lax.broadcasted_iota(
        jnp.int32, (128, 128), 1
    )
    small = 1.0 / math.sqrt(8 * NC * GW)
    for d in range(G):
        v = every[d % 2, d // 2].astype(F32) * small
        ofine[d] = jnp.where(lower, v[:, :GW], 0.0)
        ocoarse[d] = jnp.where(lower, v[:, GW:], 0.0)

    sent_all(c_in, NY * NZ)
    sent_all(c_out, NY * NZ)
    for k in range(NX):
        core_copy(k).wait_send()
        c_back(k).wait_send()
    for copy, n in (
        (x_copy, NX), (y_copy, NY), (z_copy, NZ),
        (x_small, NX), (y_small, NY), (z_small, NZ),
        (x_gain, NX), (y_gain, NY), (z_gain, NZ),
        (z_back, NZ), (y_back, NY), (x_back, NX),
    ):
        sent_all(copy, n)
    c_small().wait_send()
    c_gain().wait_send()


def vmem(n):
    return [pl.BlockSpec(memory_space=pltpu.VMEM)] * n


def dma(*shape):
    return pltpu.SemaphoreType.DMA(shape)


def norm_rows(values):
    scale_inv = lax.rsqrt(jnp.mean(values * values, axis=-1, keepdims=True) + EPS)
    return (values * scale_inv, scale_inv)


def norm_back(upstream, normed, scale_inv):
    return scale_inv * (upstream - normed * jnp.mean(upstream * normed, axis=-1, keepdims=True))


def on_device(tokens, cotangent, gain_mix, gain_mlp, fine, coarse, w_gate_up, w_down):
    tok = tokens.reshape(BL, NB, D)
    gain = gain_mix.reshape(1, D)
    S = jax.ShapeDtypeStruct
    V = pltpu.VMEM
    mixed, hid, moved, fgu, fdn = pl.pallas_call(
        forward_kernel,
        name="mix_forward",
        out_shape=(
            S((BL, NB, D), BF16),
            S((BL, NB, D), BF16),
            S((NC, BW, QW), BF16),
            S((D, 2 * FF), BF16),
            S((D, FF), BF16),
        ),
        in_specs=vmem(6),
        out_specs=tuple(vmem(5)),
        scratch_shapes=[
            V((BL, NB, D), BF16),
            V((NC, BW, QW), BF16),
            V((2, NC * BW, GW), F32),
            V((2, NC * BW, GW), F32),
            V((NZ, 4, WC), BF16),
            V((32, WC), F32),
            dma(32), dma(32), dma(32), dma(32),
            dma(8), dma(8), dma(2, 4), dma(2, 4), dma(2, 4), dma(2, 4), dma(2, 4), dma(2, 4),
        ],
        compiler_params=pltpu.CompilerParams(
            collective_id=0, has_side_effects=True, vmem_limit_bytes=60 * 1024 * 1024
        ),
    )(tok, gain, fine, coarse, w_gate_up, w_down)

    source = tokens[0].astype(F32)
    mixed32 = mixed.reshape(ROWS, D).astype(F32)
    hid32 = hid.reshape(ROWS, D).astype(F32)
    after_mix = source + mixed32 * hid32
    normed_mlp, inv_mlp = norm_rows(after_mix)
    mlp_in = (normed_mlp * gain_mlp).astype(BF16)
    both = jnp.dot(mlp_in, fgu, preferred_element_type=F32)
    gate_pre = both[:, :FF]
    upward = both[:, FF:]
    squash = jax.nn.sigmoid(gate_pre)
    silu_gate = gate_pre * squash
    silu_slope = squash * (1.0 + gate_pre * (1.0 - squash))
    act = (silu_gate * upward).astype(BF16)
    projected = dot(act, fdn, 1, 1)
    layer = (after_mix + projected).astype(BF16)
    cot = cotangent[0]
    back_act = jnp.dot(cot, fdn, preferred_element_type=F32).astype(BF16).astype(F32)
    bboth = jnp.concatenate(
        [back_act * upward * silu_slope, back_act * silu_gate], axis=1
    ).astype(BF16)
    back_mlp_in = dot(bboth, fgu, 1, 1)
    glm = jnp.sum(back_mlp_in * normed_mlp, axis=0)
    bafter = cot.astype(F32) + norm_back(back_mlp_in * gain_mlp, normed_mlp, inv_mlp)
    bm = (bafter * hid32).astype(BF16)

    gin, ogu, odn, ofine, ocoarse, ogain = pl.pallas_call(
        backward_kernel,
        name="mix_backward",
        out_shape=(
            S((BL, NB, D), BF16),
            S((4, 2 * FF), F32),
            S((4, FF), F32),
            S((G, NB, NB), F32),
            S((G, NC, NC), F32),
            S((8, 256), F32),
        ),
        in_specs=vmem(14),
        out_specs=tuple(vmem(6)),
        scratch_shapes=[
            V((NC, BW, QW), BF16),
            V((NC, BW, QW), BF16),
            V((BL, NB, D), BF16),
            V((BL, NB, D), F32),
            V((2, NC * BW, GW), F32),
            V((2, NC * BW, GW), F32),
            V((2, NC * BW, GW), F32),
            V((8, 128, WC), BF16),
            V((4, 128, WC), BF16),
            V((3, 128, WC), BF16),
            V((128, WC), F32),
            V((4, 32, WC), BF16),
            V((3, 32, WC), BF16),
            V((8, 4, WC), F32),
            V((7, 4, WC), F32),
            V((2, 4, 128, 256), F32),
            V((4, 128, 256), BF16),
            V((4, 128, 256), BF16),
            V((4, 128, 256), BF16),
            V((3, 128, 256), BF16),
            V((128, 256), F32),
            V((4, 32, 256), BF16),
            V((3, 32, 256), BF16),
            V((8, 4, 256), F32),
            V((7, 4, 256), F32),
            V((8, 4, 256), F32),
            V((32, 256), F32),
            V((4, 32, 256), BF16),
            V((2, 4, 128, 256), BF16),
            V((2, 8, 256), F32),
            V((4, 8, 256), F32),
            V((4, 8, 256), F32),
            V((8, 8, 256), F32),
            dma(32), dma(32), dma(32), dma(32),
            dma(4), dma(4), dma(4), dma(4), dma(4), dma(4), dma(8), dma(8),
            dma(8, 8), dma(8, 8), dma(4, 8), dma(4, 8),
        ],
        compiler_params=pltpu.CompilerParams(
            collective_id=1, has_side_effects=True, vmem_limit_bytes=60 * 1024 * 1024
        ),
    )(
        bm.reshape(BL, NB, D), moved, fine, coarse, mlp_in, bboth, cot, act,
        bafter.reshape(BL, NB, D), mixed, hid, tok, gain, glm.reshape(8, GW),
    )
    return (
        layer.reshape(1, ROWS, D),
        gin.reshape(1, ROWS, D),
        ogu,
        odn,
        ofine,
        ocoarse,
        ogain[:, :GW].reshape(D),
        ogain[:, GW:].reshape(D),
    )


def solution(mesh):
    rows = P("dp", "seq", None)
    weights = P(("dp", "seq"), None)
    return jax.shard_map(
        on_device,
        mesh=mesh,
        in_specs=(rows, rows, P(), P(), P(), P(), weights, weights),
        out_specs=(rows, rows, weights, weights, P(), P(), P(), P()),
        check_vma=False,
    )
```

```python
import math

import jax
import jax.numpy as jnp
from jax import lax
from jax.experimental import pallas as pl
from jax.experimental.pallas import tpu as pltpu
from jax.sharding import PartitionSpec as P

D = 1024
FF = 1024
NB = 128
NC = 128
GW = 128
G = 8
NX, NY, NZ = 4, 4, 8
BL = 4
QW = 256
BW = 16
ROWS = BL * NB
WC = 3 * FF
EPS = 1e-05
MESH = pl.DeviceIdType.MESH
F32 = jnp.float32
BF16 = jnp.bfloat16


def place():
    dp = lax.axis_index("dp")
    seq = lax.axis_index("seq")
    return dp // 2, dp % 2, seq // NZ, seq % NZ


def send(src, dst, ssem, rsem, dp, seq):
    return pltpu.make_async_remote_copy(
        src_ref=src,
        dst_ref=dst,
        send_sem=ssem,
        recv_sem=rsem,
        device_id=(dp, seq),
        device_id_type=MESH,
    )


def greet(x, c, y, z):
    bar = pltpu.get_barrier_semaphore()

    def one(dp, seq):
        pl.semaphore_signal(bar, inc=1, device_id=(dp, seq), device_id_type=MESH)

    def plane(k, carry):
        one(2 * x + c, ((y + k // NZ) % NY) * NZ + (z + k % NZ) % NZ)
        return carry

    lax.fori_loop(1, NY * NZ, plane, 0)
    for k in range(1, 2 * NX):
        one((2 * x + c + k) % (2 * NX), y * NZ + z)
    return bar, NY * NZ - 1 + 2 * NX - 1


def dot(a, b, ca=1, cb=0):
    return lax.dot_general(a, b, (((ca,), (cb,)), ((), ())), preferred_element_type=F32)


def exchange_in(src, dst, ssem, rsem, x, c, y, z):
    me = y * NZ + z

    def part(slot, first, count, lane, width):
        def copy(k):
            ty = (y + k // NZ) % NY
            tz = (z + k % NZ) % NZ
            return send(
                src.at[
                    pl.ds(first, count),
                    pl.ds(pl.multiple_of(BW * tz, BW), BW),
                    pl.ds(pl.multiple_of(QW * ty + lane, GW), width),
                ],
                dst.at[pl.ds(BL * me + first, count), :, pl.ds(lane, width)],
                ssem.at[slot, k],
                rsem.at[slot, k],
                2 * x + c,
                ty * NZ + tz,
            )

        return copy

    return part


def exchange_out(src, dst, ssem, rsem, x, c, y, z):
    def part(slot, first, count, lane, width):
        def copy(k):
            ty = (y + k // NZ) % NY
            tz = (z + k % NZ) % NZ
            to = ty * NZ + tz
            return send(
                src.at[pl.ds(BL * to + first, count), :, pl.ds(lane, width)],
                dst.at[
                    pl.ds(first, count),
                    pl.ds(pl.multiple_of(BW * z, BW), BW),
                    pl.ds(pl.multiple_of(QW * y + lane, GW), width),
                ],
                ssem.at[slot, k],
                rsem.at[slot, k],
                2 * x + c,
                to,
            )

        return copy

    return part


def start_all(copy, n):
    def body(k, carry):
        copy(k).start()
        return carry

    lax.fori_loop(1, n, body, 0)


def recv_all(copy, n):
    def body(k, carry):
        copy(k).wait_recv()
        return carry

    lax.fori_loop(1, n, body, 0)


def sent_all(copy, n):
    def body(k, carry):
        copy(k).wait_send()
        return carry

    lax.fori_loop(1, n, body, 0)


def to_rows(src, tall, h):
    def body(i, carry):
        v = src[pl.ds(8 * i, 8), :, GW * h : GW * h + GW].reshape(8 * BW, GW).astype(F32)
        tall[h, pl.ds(pl.multiple_of(8 * BW * i, 8 * BW), 8 * BW), :] = v
        return carry

    lax.fori_loop(0, NC // 8, body, 0)


def from_rows(tall, dst, h):
    def body(i, carry):
        v = tall[h, pl.ds(pl.multiple_of(8 * BW * i, 8 * BW), 8 * BW), :].astype(BF16)
        dst[pl.ds(8 * i, 8), :, GW * h : GW * h + GW] = v.reshape(8, BW, GW)
        return carry

    lax.fori_loop(0, NC // 8, body, 0)


def columns(tall, h, first, count):
    at = [tall[h, pl.ds(b, NC, stride=BW), :].astype(BF16) for b in range(first, first + count)]
    return jnp.concatenate(at, axis=1)


def coarse_mix(factor, tall, out, h, side):
    for b in range(0, BW, 4):
        v = dot(factor, columns(tall, h, b, 4), side, 0)
        for n in range(4):
            out[h, pl.ds(b + n, NC, stride=BW), :] = v[:, n * GW : n * GW + GW]


def own_in(src, dst, x, c, y, z):
    dst[pl.ds(BL * (y * NZ + z), BL)] = src[
        :, pl.ds(pl.multiple_of(BW * z, BW), BW), pl.ds(pl.multiple_of(QW * y, QW), QW)
    ]


def own_out(src, dst, x, c, y, z):
    dst[:, pl.ds(pl.multiple_of(BW * z, BW), BW), pl.ds(pl.multiple_of(QW * y, QW), QW)] = src[
        pl.ds(BL * (y * NZ + z), BL)
    ]


class SmallSum:
    def __init__(self, refs, sems, gain, x, c, y, z):
        self.v, self.vs, self.vr, self.pieces, self.pr, self.cg, self.full, self.every = refs[:8]
        self.ss, self.rs = sems
        self.gain = gain
        self.dp, self.y, self.z = 2 * x + c, y, z
        self.seq = y * NZ + z

    def plane(self, k):
        return ((self.y + k // NZ) % NY) * NZ + (self.z + k % NZ) % NZ

    def a(self, k):
        to = (self.dp + k) % 8
        return send(self.vs.at[to], self.vr.at[k], self.ss.at[0, k], self.rs.at[0, k], to, self.seq)

    def ga(self, k):
        to = (self.dp + k) % 8
        loc, rec, _, _, gs, gr = self.gain
        return send(loc.at[to], rec.at[k], gs.at[0, k], gr.at[0, k], to, self.seq)

    def b(self, k):
        to = self.plane(k)
        return send(
            self.pieces.at[to], self.pr.at[k], self.ss.at[1, k], self.rs.at[1, k], self.dp, to
        )

    def c(self, k):
        return send(
            self.cg.at[self.seq], self.cg.at[self.seq],
            self.ss.at[2, k], self.rs.at[2, k], self.dp, self.plane(k),
        )

    def d(self, k):
        to = (self.dp + k) % 8
        return send(
            self.every.at[self.dp], self.every.at[self.dp],
            self.ss.at[3, k], self.rs.at[3, k], to, self.seq,
        )

    def gd(self, k):
        to = (self.dp + k) % 8
        _, _, _, ge, gs, gr = self.gain
        return send(ge.at[self.dp], ge.at[self.dp], gs.at[1, k], gr.at[1, k], to, self.seq)

    def start_a(self):
        if self.gain is not None:
            start_all(self.ga, 8)
        for d in range(G):
            self.vs[d] = self.v[d].astype(BF16)
        start_all(self.a, 8)

    def start_b(self):
        if self.gain is not None:
            recv_all(self.ga, 8)
            t = self.gain[0][self.dp]
            for k in range(1, 8):
                t = t + self.gain[1][k]
        recv_all(self.a, 8)
        s = self.v[self.dp]
        for k in range(1, 8):
            s = s + self.vr[k].astype(F32)
        for j in range(NY * NZ):
            self.pieces[j, :4, :] = s[4 * j : 4 * j + 4]
            if self.gain is not None:
                self.pieces[j, 4:, :] = t[:4]
            else:
                self.pieces[j, 4:, :] = jnp.zeros((4, 128), F32)
        start_all(self.b, NY * NZ)

    def start_c(self):
        recv_all(self.b, NY * NZ)
        s = self.pieces[self.seq]
        for k in range(1, NY * NZ):
            s = s + self.pr[k]
        self.cg[self.seq] = s
        start_all(self.c, NY * NZ)

    def start_d(self):
        recv_all(self.c, NY * NZ)
        if self.gain is not None:
            self.gain[3][self.dp] = self.cg[0]
            start_all(self.gd, 8)
        for j in range(NY * NZ):
            self.full[4 * j : 4 * j + 4, :] = self.cg[j, :4, :]
        self.every[self.dp] = self.full[...].astype(BF16)
        start_all(self.d, 8)

    def finish(self):
        recv_all(self.d, 8)
        sent_all(self.a, 8)
        sent_all(self.b, NY * NZ)
        sent_all(self.c, NY * NZ)
        sent_all(self.d, 8)
        if self.gain is not None:
            recv_all(self.gd, 8)
            sent_all(self.ga, 8)
            sent_all(self.gd, 8)


def small_scratch():
    V = pltpu.VMEM
    return [
        V((8, 128, 128), F32),
        V((8, 128, 128), BF16),
        V((8, 128, 128), BF16),
        V((32, 8, 128), F32),
        V((32, 8, 128), F32),
        V((32, 8, 128), F32),
        V((128, 128), F32),
        dma(4, 32),
        dma(4, 32),
    ]


def dma(*shape):
    return pltpu.SemaphoreType.DMA(shape)


def blocks(ref, cols):
    return jnp.concatenate([ref[a, :, cols] for a in range(BL)], axis=1)


def layer_kernel(
    tok, cot, gain, gain2, fine, coarse, wgu, wdn,
    gin, layer, wsum, fevery, cevery, gevery,
    hid, fm, moved, back, mixed, bm, xin, xout, bfine, bhid, tall, tall2, tallm,
    wz, wrow, w,
    after, invs, mlp_in, act, bboth, bmi, glm8,
    pbuf, crecv, xrecv, acc, ysend, yrecv, zbuf, zrecv,
    s_a, r_a, s_b, r_b, s_d, r_d, s_e, r_e,
    s_g, r_g, s_c, r_c, s_x, r_x, s_y, r_y, s_z, r_z,
    gloc, grec, gs, gr,
    *small,
):
    x, c, y, z = place()
    dp = 2 * x + c
    seq = y * NZ + z
    sib = 2 * x + 1 - c
    bar, count = greet(x, c, y, z)
    sf = SmallSum((*small[:7], fevery), small[7:9], (gloc, grec, None, gevery, gs, gr), x, c, y, z)
    sc = SmallSum((*small[9:16], cevery), small[16:18], None, x, c, y, z)

    wz[pl.ds(z, 1), :, : 2 * FF] = wgu[...].reshape(1, 4, 2 * FF)
    wz[pl.ds(z, 1), :, 2 * FF :] = wdn[...].reshape(1, 4, FF)
    HA = slice(0, WC // 2)
    HB = slice(WC // 2, WC)

    def gz(k):
        tz = (z + k) % NZ
        return send(wz.at[z], wz.at[z], s_g.at[0, k], r_g.at[0, k], dp, y * NZ + tz)

    def ga_y(k):
        at = w.at[x, c, y, :, HA]
        return send(at, at, s_g.at[1, k], r_g.at[1, k], dp, ((y + k) % NY) * NZ + z)

    def ga_x(k):
        at = w.at[x, c, :, :, HA]
        return send(at, at, s_g.at[2, k], r_g.at[2, k], 2 * ((x + k) % NX) + c, seq)

    def ga_c(k):
        at = w.at[(x + NX - k) % NX, c, :, :, HA]
        return send(at, at, s_g.at[3, k], r_g.at[3, k], sib, seq)

    def gb_x(k):
        at = w.at[x, c, y, :, HB]
        return send(at, at, s_g.at[4, k], r_g.at[4, k], 2 * ((x + k) % NX) + c, seq)

    def gb_y(k):
        at = w.at[:, c, y, :, HB]
        return send(at, at, s_g.at[5, k], r_g.at[5, k], dp, ((y + k) % NY) * NZ + z)

    def gb_c(k):
        at = w.at[:, c, (y + NY - k) % NY, :, HB]
        return send(at, at, s_g.at[6, k], r_g.at[6, k], sib, seq)

    def norm(i, carry):
        a = i // 4
        at = pl.ds(pl.multiple_of((i % 4) * 32, 32), 32)
        v = tok[a, at, :].astype(F32)
        inv = lax.rsqrt(jnp.mean(v * v, axis=-1, keepdims=True) + EPS)
        hid[a, at, :] = ((v * inv) * gain[...]).astype(BF16)
        return carry

    lax.fori_loop(0, BL * 4, norm, 0)
    pl.semaphore_wait(bar, count)
    start_all(gz, NZ)

    ex_a = exchange_in(fm, moved, s_a, r_a, x, c, y, z)
    for h in range(2):
        for g in range(h, G, 2):
            cols = slice(g * GW, (g + 1) * GW)
            v = dot(fine[g], blocks(hid, cols)).astype(BF16)
            for a in range(BL):
                fm[a, :, cols] = v[:, a * NB : a * NB + NB]
        start_all(ex_a(h, 0, BL, GW * h, GW), NY * NZ)
    own_in(fm, moved, x, c, y, z)

    recv_all(gz, NZ)
    for zz in range(NZ):
        wrow[4 * zz : 4 * zz + 4, :] = wz[zz].astype(F32)
    w[x, c, y] = wrow[...].astype(BF16)
    start_all(ga_y, NY)
    start_all(gb_x, NX)
    recv_all(ga_y, NY)
    start_all(ga_x, NX)
    recv_all(gb_x, NX)
    start_all(gb_y, NY)
    ga_c(0).start()
    gb_c(0).start()

    for h in range(2):
        recv_all(ex_a(h, 0, BL, GW * h, GW), NY * NZ)
        to_rows(moved, tallm, h)
        coarse_mix(coarse[2 * y + h], tallm, tall2, h, 1)
        from_rows(tall2, back, h)
    ex_b = exchange_out(back, mixed, s_b, r_b, x, c, y, z)
    start_all(ex_b(0, 0, 2, 0, QW), NY * NZ)
    start_all(ex_b(1, 2, 2, 0, QW), NY * NZ)
    own_out(back, mixed, x, c, y, z)

    def gather_x(k, carry):
        ga_x(k).wait_recv()
        ga_c(k).start()
        gb_y(k).wait_recv()
        gb_c(k).start()
        return carry

    lax.fori_loop(1, NX, gather_x, 0)
    for k in range(NX):
        ga_c(k).wait_recv()
        gb_c(k).wait_recv()

    glm8[...] = jnp.zeros_like(glm8)
    ex_d = exchange_in(bm, xin, s_d, r_d, x, c, y, z)
    HALF = ROWS // 2

    def mlp(i, carry):
        rows = pl.ds(pl.multiple_of(i * HALF, HALF), HALF)
        recv_all(ex_b(i, 2 * i, 2, 0, QW), NY * NZ)

        def pre(r, carry):
            a = 2 * i + r // 8
            at = pl.ds(pl.multiple_of((r % 8) * 16, 16), 16)
            to = pl.ds(pl.multiple_of(i * HALF + r * 16, 16), 16)
            v = tok[a, at, :].astype(F32) + mixed[a, at, :].astype(F32) * hid[a, at, :].astype(F32)
            inv = lax.rsqrt(jnp.mean(v * v, axis=-1, keepdims=True) + EPS)
            after[to, :] = v
            invs[to, :] = jnp.broadcast_to(inv, (16, 128))
            mlp_in[to, :] = ((v * inv) * gain2[...]).astype(BF16)
            return carry

        lax.fori_loop(0, HALF // 16, pre, 0)

        def hidden(n, carry):
            lane = pl.multiple_of(n * 256, 256)
            cols = pl.ds(lane, 256)
            cols2 = pl.ds(pl.multiple_of(FF + lane, 256), 256)
            cols3 = pl.ds(pl.multiple_of(2 * FF + lane, 256), 256)
            m = mlp_in[rows, :]
            gate = dot(m, w[:, :, :, :, cols].reshape(D, 256))
            up = dot(m, w[:, :, :, :, cols2].reshape(D, 256))
            ba = dot(cot[rows, :], w[:, :, :, :, cols3].reshape(D, 256)).astype(BF16).astype(F32)
            sq = jax.nn.sigmoid(gate)
            sg = gate * sq
            act[rows, cols] = (sg * up).astype(BF16)
            bboth[rows, cols] = (ba * up * (sq * (1.0 + gate * (1.0 - sq)))).astype(BF16)
            bboth[rows, cols2] = (ba * sg).astype(BF16)
            return carry

        lax.fori_loop(0, FF // 256, hidden, 0)

        def up_back(m, carry):
            cols = pl.ds(pl.multiple_of(m * 256, 256), 256)
            bmi[rows, cols] = dot(bboth[rows, :], w[m, :, :, :, : 2 * FF].reshape(256, 2 * FF), 1, 1)
            return carry

        lax.fori_loop(0, D // 256, up_back, 0)

        def post(r, total):
            a = 2 * i + r // 8
            at = pl.ds(pl.multiple_of((r % 8) * 16, 16), 16)
            to = pl.ds(pl.multiple_of(i * HALF + r * 16, 16), 16)
            inv = invs[to, 0:1]
            n2 = after[to, :] * inv
            v = bmi[to, :]
            prod = v * n2
            w2 = v * gain2[...]
            center = jnp.mean(w2 * n2, axis=-1, keepdims=True)
            ba = cot[to, :].astype(F32) + inv * (w2 - n2 * center)
            bmi[to, :] = ba
            bm[a, at, :] = (ba * hid[a, at, :].astype(F32)).astype(BF16)
            return total + prod[:8] + prod[8:]

        glm8[...] = lax.fori_loop(0, HALF // 16, post, glm8[...])

        @pl.when(i == 0)
        def _():
            start_all(ex_d(0, 0, 2, 0, QW), NY * NZ)

        return carry

    lax.fori_loop(0, 2, mlp, 0)
    for h in range(2):
        start_all(ex_d(1 + h, 2, 2, GW * h, GW), NY * NZ)
    own_in(bm, xin, x, c, y, z)

    def part(d, put):
        at = pl.ds(pl.multiple_of(d * 128, 128), 128)
        lhs = mlp_in[:, at]
        for n in range(4):
            cols = slice(512 * n, 512 * n + 512)
            put(cols, dot(lhs, bboth[:, cols], 0, 0))
        lhs = cot[:, at]
        for n in range(2):
            cols = slice(512 * n, 512 * n + 512)
            put(slice(2 * FF + 512 * n, 2 * FF + 512 * n + 512), dot(lhs, act[:, cols], 0, 0))

    def core_copy(k):
        d = 2 * ((x + k) % NX) + 1 - c
        return send(pbuf.at[d], crecv.at[k], s_c.at[k], r_c.at[k], sib, seq)

    def x_copy(k):
        xx = (x + k) % NX
        return send(pbuf.at[2 * xx + c], xrecv.at[k - 1], s_x.at[k], r_x.at[k], 2 * xx + c, seq)

    def first(i, carry):
        k = (i + 1) % NX
        d = 2 * ((x + k) % NX) + 1 - c

        def put(cols, v):
            pbuf[d, :, cols] = v.astype(BF16)

        part(d, put)
        core_copy(k).start()
        return carry

    lax.fori_loop(0, NX, first, 0)

    def second(k, carry):
        d = 2 * ((x + k) % NX) + c
        core_copy(k).wait_recv()

        def put(cols, v):
            pbuf[d, :, cols] = (v + crecv[k, :, cols].astype(F32)).astype(BF16)

        part(d, put)
        x_copy(k).start()
        return carry

    lax.fori_loop(1, NX, second, 0)

    recv_all(ex_d(0, 0, 2, 0, QW), NY * NZ)
    ex_e = exchange_out(xout, bfine, s_e, r_e, x, c, y, z)
    for h in range(2):
        recv_all(ex_d(1 + h, 2, 2, GW * h, GW), NY * NZ)
        to_rows(xin, tall, h)
        coarse_mix(coarse[2 * y + h], tall, tall2, h, 0)
        from_rows(tall2, xout, h)
        start_all(ex_e(h, 0, BL, GW * h, GW), NY * NZ)
    own_out(xout, bfine, x, c, y, z)

    for d in range(G):
        sc.v[d] = jnp.zeros((NC, NC), F32)
    for h in range(2):
        total = jnp.zeros((NC, NC), F32)
        for b in range(0, BW, 4):
            total = total + dot(columns(tall, h, b, 4), columns(tallm, h, b, 4), 1, 1)
        sc.v[2 * y + h] = total
    sc.start_a()

    core_copy(0).wait_recv()

    def put_own(cols, v):
        acc[:, cols] = v + crecv[0, :, cols].astype(F32)

    part(dp, put_own)
    sc.start_b()

    def project(m, carry):
        cols = pl.ds(pl.multiple_of(m * 256, 256), 256)
        v = dot(act[...], w[m, :, :, :, 2 * FF :].reshape(256, FF), 1, 1)
        layer[:, cols] = (after[:, cols] + v).astype(BF16)
        return carry

    lax.fori_loop(0, D // 256, project, 0)
    sc.start_c()

    def y_copy(k):
        yy = (y + k) % NY
        return send(ysend.at[yy], yrecv.at[k - 1], s_y.at[k], r_y.at[k], dp, yy * NZ + z)

    def z_copy(k):
        zz = (z + k) % NZ
        return send(zbuf.at[zz], zrecv.at[k - 1], s_z.at[k], r_z.at[k], dp, y * NZ + zz)

    def weights_y():
        for k in range(1, NX):
            x_copy(k).wait_recv()

        def add_x(i, carry):
            at = pl.ds(pl.multiple_of(i * 16, 16), 16)
            v = acc[at, :]
            for k in range(NX - 1):
                v = v + xrecv[k, at, :].astype(F32)
            acc[at, :] = v
            return carry

        lax.fori_loop(0, 8, add_x, 0)
        for yy in range(NY):
            ysend[yy] = acc[32 * yy : 32 * yy + 32, :].astype(BF16)
        start_all(y_copy, NY)

    def weights_z():
        recv_all(y_copy, NY)
        for q in range(4):
            at = pl.ds(pl.multiple_of(32 * y + 8 * q, 8), 8)
            v = acc[at, :]
            for k in range(NY - 1):
                v = v + yrecv[k, 8 * q : 8 * q + 8, :].astype(F32)
            zbuf[2 * q] = v[:4]
            zbuf[2 * q + 1] = v[4:]
        start_all(z_copy, NZ)

    def last_mix(h):
        recv_all(ex_e(h, 0, BL, GW * h, GW), NY * NZ)
        for g in range(h, G, 2):
            cols = slice(g * GW, (g + 1) * GW)
            v = blocks(bfine, cols)
            sf.v[g] = dot(v, blocks(hid, cols), 1, 1)
            v = dot(fine[g], v, 0, 0)
            for a in range(BL):
                bhid[a, :, cols] = (
                    bmi[a * NB : a * NB + NB, cols] * mixed[a, :, cols].astype(F32)
                    + v[:, a * NB : a * NB + NB]
                )

    last_mix(0)
    last_mix(1)

    def sums(i, total):
        a = i // 8
        at = pl.ds(pl.multiple_of((i % 8) * 16, 16), 16)
        v = tok[a, at, :].astype(F32)
        inv = lax.rsqrt(jnp.mean(v * v, axis=-1, keepdims=True) + EPS)
        prod = bhid[a, at, :] * (v * inv)
        return total + prod[:8] + prod[8:]

    gm = lax.fori_loop(0, BL * 8, sums, jnp.zeros((8, D), F32))
    gm = jnp.sum(gm, axis=0, keepdims=True)
    gl = jnp.sum(glm8[...], axis=0, keepdims=True)
    for d in range(G):
        gloc[d, 0:1, :] = gm[:, d * GW : (d + 1) * GW]
        gloc[d, 1:2, :] = gl[:, d * GW : (d + 1) * GW]
        gloc[d, 2:, :] = jnp.zeros((6, GW), F32)
    sf.start_a()
    weights_y()
    sf.start_b()

    def last(i, carry):
        a = i // 8
        at = pl.ds(pl.multiple_of((i % 8) * 16, 16), 16)
        to = pl.ds(pl.multiple_of(i * 16, 16), 16)
        v = tok[a, at, :].astype(F32)
        inv = lax.rsqrt(jnp.mean(v * v, axis=-1, keepdims=True) + EPS)
        normed = v * inv
        w1 = bhid[a, at, :] * gain[...]
        center = jnp.mean(w1 * normed, axis=-1, keepdims=True)
        gin[a, at, :] = (bmi[to, :] + inv * (w1 - normed * center)).astype(BF16)
        return carry

    lax.fori_loop(0, BL * 8, last, 0)
    sf.start_c()
    weights_z()
    sc.start_d()
    sf.start_d()
    recv_all(z_copy, NZ)
    v = zbuf[z]
    for k in range(NZ - 1):
        v = v + zrecv[k]
    wsum[...] = v

    sent_all(gz, NZ)
    for copy in (ga_y, ga_x, gb_x, gb_y, x_copy, y_copy):
        sent_all(copy, 4)
    for k in range(NX):
        ga_c(k).wait_send()
        gb_c(k).wait_send()
        core_copy(k).wait_send()
    sent_all(z_copy, NZ)
    for h in range(2):
        sent_all(ex_a(h, 0, BL, GW * h, GW), NY * NZ)
        sent_all(ex_b(h, 2 * h, 2, 0, QW), NY * NZ)
        sent_all(ex_d(1 + h, 2, 2, GW * h, GW), NY * NZ)
        sent_all(ex_e(h, 0, BL, GW * h, GW), NY * NZ)
    sent_all(ex_d(0, 0, 2, 0, QW), NY * NZ)
    sc.finish()
    sf.finish()


def finish_kernel(
    gin, layer, wsum, fevery, cevery, gevery,
    ogin, olayer, ogu, odn, ofine, ocoarse, omix, omlp,
):
    olayer[0] = layer[...]
    ogin[0] = gin[...].reshape(ROWS, D)
    scale = 1.0 / math.sqrt(8 * NC * NB)
    ogu[...] = wsum[:, : 2 * FF] * scale
    odn[...] = wsum[:, 2 * FF :] * scale
    lower = lax.broadcasted_iota(jnp.int32, (128, 128), 0) >= lax.broadcasted_iota(
        jnp.int32, (128, 128), 1
    )
    small = 1.0 / math.sqrt(8 * NC * GW)
    for d in range(G):
        ofine[d] = jnp.where(lower, fevery[d].astype(F32) * small, 0.0)
        ocoarse[d] = jnp.where(lower, cevery[d].astype(F32) * small, 0.0)
        omix[:, d * GW : (d + 1) * GW] = gevery[d, 4:5, :] * scale
        omlp[:, d * GW : (d + 1) * GW] = gevery[d, 5:6, :] * scale


def vmem(n):
    return [pl.BlockSpec(memory_space=pltpu.VMEM)] * n


def on_device(tokens, cotangent, gain_mix, gain_mlp, fine, coarse, w_gate_up, w_down):
    S = jax.ShapeDtypeStruct
    V = pltpu.VMEM
    parts = pl.pallas_call(
        layer_kernel,
        name="layer",
        out_shape=(
            S((BL, NB, D), BF16),
            S((ROWS, D), BF16),
            S((4, WC), F32),
            S((G, 128, 128), BF16),
            S((G, 128, 128), BF16),
            S((G, 8, 128), F32),
        ),
        in_specs=vmem(8),
        out_specs=tuple(vmem(6)),
        scratch_shapes=[
            V((BL, NB, D), BF16),
            V((BL, NB, D), BF16),
            V((NC, BW, QW), BF16),
            V((NC, BW, QW), BF16),
            V((BL, NB, D), BF16),
            V((BL, NB, D), BF16),
            V((NC, BW, QW), BF16),
            V((NC, BW, QW), BF16),
            V((BL, NB, D), BF16),
            V((BL, NB, D), F32),
            V((2, NC * BW, GW), F32),
            V((2, NC * BW, GW), F32),
            V((2, NC * BW, GW), F32),
            V((NZ, 4, WC), BF16),
            V((32, WC), F32),
            V((NX, 2, NY, 32, WC), BF16),
            V((ROWS, D), F32),
            V((ROWS, 128), F32),
            V((ROWS, D), BF16),
            V((ROWS, FF), BF16),
            V((ROWS, 2 * FF), BF16),
            V((ROWS, D), F32),
            V((8, D), F32),
            V((8, 128, WC), BF16),
            V((4, 128, WC), BF16),
            V((3, 128, WC), BF16),
            V((128, WC), F32),
            V((4, 32, WC), BF16),
            V((3, 32, WC), BF16),
            V((8, 4, WC), F32),
            V((7, 4, WC), F32),
            dma(2, 32), dma(2, 32), dma(2, 32), dma(2, 32),
            dma(3, 32), dma(3, 32), dma(2, 32), dma(2, 32),
            dma(7, 8), dma(7, 8),
            dma(4), dma(4), dma(4), dma(4), dma(4), dma(4), dma(8), dma(8),
            V((8, 8, 128), F32), V((8, 8, 128), F32), dma(2, 8), dma(2, 8),
            *small_scratch(), *small_scratch(),
        ],
        compiler_params=pltpu.CompilerParams(
            collective_id=0, has_side_effects=True, vmem_limit_bytes=63 * 1024 * 1024
        ),
    )(
        tokens.reshape(BL, NB, D), cotangent.reshape(ROWS, D),
        gain_mix.reshape(1, D), gain_mlp.reshape(1, D), fine, coarse, w_gate_up, w_down,
    )
    gin, layer, ogu, odn, ofine, ocoarse, omix, omlp = pl.pallas_call(
        finish_kernel,
        name="finish",
        out_shape=(
            S((1, ROWS, D), BF16),
            S((1, ROWS, D), BF16),
            S((4, 2 * FF), F32),
            S((4, FF), F32),
            S((G, NB, NB), F32),
            S((G, NC, NC), F32),
            S((1, D), F32),
            S((1, D), F32),
        ),
        in_specs=vmem(6),
        out_specs=tuple(vmem(8)),
    )(*parts)
    return (layer, gin, ogu, odn, ofine, ocoarse, omix.reshape(D), omlp.reshape(D))


def solution(mesh):
    rows = P("dp", "seq", None)
    weights = P(("dp", "seq"), None)
    return jax.shard_map(
        on_device,
        mesh=mesh,
        in_specs=(rows, rows, P(), P(), P(), P(), weights, weights),
        out_specs=(rows, rows, weights, weights, P(), P(), P(), P()),
        check_vma=False,
    )
```

```python
import math

import jax
import jax.numpy as jnp
from jax import lax
from jax.experimental import pallas as pl
from jax.experimental.pallas import tpu as pltpu
from jax.sharding import PartitionSpec as P

D = 1024
FF = 1024
NB = 128
NC = 128
GW = 128
G = 8
NX, NY, NZ = 4, 4, 8
BL = 4
QW = 256
BW = 16
ROWS = BL * NB
WC = 3 * FF
EPS = 1e-05
MESH = pl.DeviceIdType.MESH
F32 = jnp.float32
BF16 = jnp.bfloat16


def place():
    dp = lax.axis_index("dp")
    seq = lax.axis_index("seq")
    return lax.div(dp, 2), lax.rem(dp, 2), lax.div(seq, NZ), lax.rem(seq, NZ)


def shifted(y, z, k):
    return lax.rem(y + lax.div(k, NZ), NY), lax.rem(z + lax.rem(k, NZ), NZ)


def send(src, dst, ssem, rsem, dp, seq):
    return pltpu.make_async_remote_copy(
        src_ref=src,
        dst_ref=dst,
        send_sem=ssem,
        recv_sem=rsem,
        device_id=(dp, seq),
        device_id_type=MESH,
    )


def greet(x, c, y, z):
    bar = pltpu.get_barrier_semaphore()

    def one(dp, seq):
        pl.semaphore_signal(bar, inc=1, device_id=(dp, seq), device_id_type=MESH)

    def plane(k, carry):
        ty, tz = shifted(y, z, k)
        one(2 * x + c, ty * NZ + tz)
        return carry

    lax.fori_loop(1, NY * NZ, plane, 0)
    for k in range(1, 2 * NX):
        one((2 * x + c + k) % (2 * NX), y * NZ + z)
    return bar, NY * NZ - 1 + 2 * NX - 1


def dot(a, b, ca=1, cb=0):
    return lax.dot_general(a, b, (((ca,), (cb,)), ((), ())), preferred_element_type=F32)


def exchange_in(src, dst, ssem, rsem, x, c, y, z):
    me = y * NZ + z

    def part(slot, first, count, lane, width):
        def copy(k):
            ty, tz = shifted(y, z, k)
            return send(
                src.at[
                    pl.ds(first, count),
                    pl.ds(pl.multiple_of(BW * tz, BW), BW),
                    pl.ds(pl.multiple_of(QW * ty + lane, GW), width),
                ],
                dst.at[pl.ds(BL * me + first, count), :, pl.ds(lane, width)],
                ssem.at[slot],
                rsem.at[slot],
                2 * x + c,
                ty * NZ + tz,
            )

        seen = dst.at[pl.ds(0, count * (NY * NZ - 1)), :, pl.ds(lane, width)]
        copy.recv = lambda: bulk(seen, rsem.at[slot])
        copy.sent = lambda: bulk(seen, ssem.at[slot])
        return copy

    return part


def exchange_out(src, dst, ssem, rsem, x, c, y, z):
    def part(slot, first, count, lane, width):
        def copy(k):
            ty, tz = shifted(y, z, k)
            to = ty * NZ + tz
            return send(
                src.at[pl.ds(BL * to + first, count), :, pl.ds(lane, width)],
                dst.at[
                    pl.ds(first, count),
                    pl.ds(pl.multiple_of(BW * z, BW), BW),
                    pl.ds(pl.multiple_of(QW * y + lane, GW), width),
                ],
                ssem.at[slot],
                rsem.at[slot],
                2 * x + c,
                to,
            )

        seen = src.at[pl.ds(0, count * (NY * NZ - 1)), :, pl.ds(lane, width)]
        copy.recv = lambda: bulk(seen, rsem.at[slot])
        copy.sent = lambda: bulk(seen, ssem.at[slot])
        return copy

    return part


def bulk(ref, sem):
    pltpu.make_async_copy(ref, ref, sem).wait()


def start_all(copy, n):
    def body(k, carry):
        copy(k).start()
        return carry

    lax.fori_loop(1, n, body, 0)


def recv_all(copy, n):
    def body(k, carry):
        copy(k).wait_recv()
        return carry

    lax.fori_loop(1, n, body, 0)


def sent_all(copy, n):
    def body(k, carry):
        copy(k).wait_send()
        return carry

    lax.fori_loop(1, n, body, 0)


def to_rows(src, tall, h):
    def body(i, carry):
        v = src[pl.ds(8 * i, 8), :, GW * h : GW * h + GW].reshape(8 * BW, GW).astype(F32)
        tall[h, pl.ds(pl.multiple_of(8 * BW * i, 8 * BW), 8 * BW), :] = v
        return carry

    lax.fori_loop(0, NC // 8, body, 0)


def from_rows(tall, dst, h):
    def body(i, carry):
        v = tall[h, pl.ds(pl.multiple_of(8 * BW * i, 8 * BW), 8 * BW), :].astype(BF16)
        dst[pl.ds(8 * i, 8), :, GW * h : GW * h + GW] = v.reshape(8, BW, GW)
        return carry

    lax.fori_loop(0, NC // 8, body, 0)


def columns(tall, h, first, count):
    at = [tall[h, pl.ds(b, NC, stride=BW), :].astype(BF16) for b in range(first, first + count)]
    return jnp.concatenate(at, axis=1)


def coarse_mix(factor, tall, out, h, side):
    for b in range(0, BW, 4):
        v = dot(factor, columns(tall, h, b, 4), side, 0)
        for n in range(4):
            out[h, pl.ds(b + n, NC, stride=BW), :] = v[:, n * GW : n * GW + GW]


def own_in(src, dst, x, c, y, z):
    dst[pl.ds(BL * (y * NZ + z), BL)] = src[
        :, pl.ds(pl.multiple_of(BW * z, BW), BW), pl.ds(pl.multiple_of(QW * y, QW), QW)
    ]


def own_out(src, dst, x, c, y, z):
    dst[:, pl.ds(pl.multiple_of(BW * z, BW), BW), pl.ds(pl.multiple_of(QW * y, QW), QW)] = src[
        pl.ds(BL * (y * NZ + z), BL)
    ]


class SmallSum:
    def __init__(self, refs, sems, gain, x, c, y, z):
        self.v, self.vs, self.vr, self.pieces, self.pr, self.cg, self.full, self.every = refs[:8]
        self.ss, self.rs = sems
        self.gain = gain
        self.dp, self.y, self.z = 2 * x + c, y, z
        self.seq = y * NZ + z

    def plane(self, k):
        ty, tz = shifted(self.y, self.z, k)
        return ty * NZ + tz

    def a(self, k):
        to = lax.rem(self.dp + k, 8)
        return send(self.vs.at[to], self.vr.at[k], self.ss.at[0], self.rs.at[0], to, self.seq)

    def ga(self, k):
        to = lax.rem(self.dp + k, 8)
        loc, rec, _, _, gs, gr = self.gain
        return send(loc.at[to], rec.at[k], gs.at[0], gr.at[0], to, self.seq)

    def b(self, k):
        to = self.plane(k)
        return send(
            self.pieces.at[to], self.pr.at[k], self.ss.at[1], self.rs.at[1], self.dp, to
        )

    def c(self, k):
        return send(
            self.cg.at[self.seq], self.cg.at[self.seq],
            self.ss.at[2], self.rs.at[2], self.dp, self.plane(k),
        )

    def d(self, k):
        to = lax.rem(self.dp + k, 8)
        return send(
            self.every.at[self.dp], self.every.at[self.dp],
            self.ss.at[3], self.rs.at[3], to, self.seq,
        )

    def gd(self, k):
        to = lax.rem(self.dp + k, 8)
        _, _, _, ge, gs, gr = self.gain
        return send(ge.at[self.dp], ge.at[self.dp], gs.at[1], gr.at[1], to, self.seq)

    def start_a(self):
        for d in range(G):
            self.vs[d] = self.v[d].astype(BF16)
        start_all(self.a, 8)

    def start_gain(self):
        start_all(self.ga, 8)

    def start_b(self):
        bulk(self.vr.at[pl.ds(1, 7)], self.rs.at[0])
        s = self.v[self.dp]
        for k in range(1, 8):
            s = s + self.vr[k].astype(F32)
        if self.gain is not None:
            loc, rec, _, _, gs, gr = self.gain
            bulk(rec.at[pl.ds(1, 7)], gr.at[0])
            t = loc[self.dp]
            for k in range(1, 8):
                t = t + rec[k]
            t = t[:4]
        else:
            t = jnp.zeros((4, 128), F32)
        for j in range(NY * NZ):
            self.pieces[j, :4, :] = s[4 * j : 4 * j + 4]
            self.pieces[j, 4:, :] = t
        start_all(self.b, NY * NZ)

    def start_c(self):
        bulk(self.pr.at[pl.ds(1, NY * NZ - 1)], self.rs.at[1])
        s = self.pieces[self.seq]
        for k in range(1, NY * NZ):
            s = s + self.pr[k]
        self.cg[self.seq] = s
        start_all(self.c, NY * NZ)

    def start_d(self):
        bulk(self.cg.at[pl.ds(0, NY * NZ - 1)], self.rs.at[2])
        if self.gain is not None:
            self.gain[3][self.dp] = self.cg[0]
            start_all(self.gd, 8)
        for j in range(NY * NZ):
            self.full[4 * j : 4 * j + 4, :] = self.cg[j, :4, :]
        self.every[self.dp] = self.full[...].astype(BF16)
        start_all(self.d, 8)

    def finish(self):
        bulk(self.every.at[pl.ds(0, 7)], self.rs.at[3])
        bulk(self.vs.at[pl.ds(0, 7)], self.ss.at[0])
        bulk(self.pieces.at[pl.ds(0, NY * NZ - 1)], self.ss.at[1])
        bulk(self.cg.at[pl.ds(0, NY * NZ - 1)], self.ss.at[2])
        bulk(self.every.at[pl.ds(0, 7)], self.ss.at[3])
        if self.gain is not None:
            loc, _, _, ge, gs, gr = self.gain
            bulk(ge.at[pl.ds(0, 7)], gr.at[1])
            bulk(loc.at[pl.ds(0, 7)], gs.at[0])
            bulk(ge.at[pl.ds(0, 7)], gs.at[1])


def small_scratch():
    V = pltpu.VMEM
    return [
        V((8, 128, 128), F32),
        V((8, 128, 128), BF16),
        V((8, 128, 128), BF16),
        V((32, 8, 128), F32),
        V((32, 8, 128), F32),
        V((32, 8, 128), F32),
        V((128, 128), F32),
        dma(4),
        dma(4),
    ]


def dma(*shape):
    return pltpu.SemaphoreType.DMA(shape)


def blocks(ref, cols):
    return jnp.concatenate([ref[a, :, cols] for a in range(BL)], axis=1)


def layer_kernel(
    tok, cot, gain, gain2, fine, coarse, wgu, wdn,
    gin, layer, wsum, fevery, cevery, gevery,
    hid, fm, moved, back, mixed, bm, xin, xout, bfine, bhid, tall, tall2, tallm,
    wz, wrow, w,
    after, invs, mlp_in, act, bboth, bmi, glm8,
    pbuf, crecv, xrecv, brecv, acc, accb, ysend, bsend, yrecv, bxrecv, zbuf, zrecv,
    s_a, r_a, s_b, r_b, s_d, r_d, s_e, r_e,
    s_g, r_g, s_c, r_c, s_x, r_x, s_y, r_y, s_z, r_z,
    gloc, grec, gs, gr,
    *small,
):
    x, c, y, z = place()
    dp = 2 * x + c
    seq = y * NZ + z
    sib = 2 * x + 1 - c
    bar, count = greet(x, c, y, z)
    sf = SmallSum((*small[:7], fevery), small[7:9], (gloc, grec, None, gevery, gs, gr), x, c, y, z)
    sc = SmallSum((*small[9:16], cevery), small[16:18], None, x, c, y, z)

    wz[pl.ds(z, 1), :, : 2 * FF] = wgu[...].reshape(1, 4, 2 * FF)
    wz[pl.ds(z, 1), :, 2 * FF :] = wdn[...].reshape(1, 4, FF)
    HA = slice(0, WC // 2)
    HB = slice(WC // 2, WC)

    def gz(k):
        tz = (z + k) % NZ
        return send(wz.at[z], wz.at[z], s_g.at[0, k], r_g.at[0, k], dp, y * NZ + tz)

    def ga_y(k):
        at = w.at[x, c, y, :, HA]
        return send(at, at, s_g.at[1, k], r_g.at[1, k], dp, ((y + k) % NY) * NZ + z)

    def ga_x(k):
        at = w.at[x, c, :, :, HA]
        return send(at, at, s_g.at[2, k], r_g.at[2, k], 2 * ((x + k) % NX) + c, seq)

    def ga_c(k):
        at = w.at[(x + NX - k) % NX, c, :, :, HA]
        return send(at, at, s_g.at[3, k], r_g.at[3, k], sib, seq)

    def gb_x(k):
        at = w.at[x, c, y, :, HB]
        return send(at, at, s_g.at[4, k], r_g.at[4, k], 2 * ((x + k) % NX) + c, seq)

    def gb_y(k):
        at = w.at[:, c, y, :, HB]
        return send(at, at, s_g.at[5, k], r_g.at[5, k], dp, ((y + k) % NY) * NZ + z)

    def gb_c(k):
        at = w.at[:, c, (y + NY - k) % NY, :, HB]
        return send(at, at, s_g.at[6, k], r_g.at[6, k], sib, seq)

    def norm(i, carry):
        a = i // 4
        at = pl.ds(pl.multiple_of((i % 4) * 32, 32), 32)
        v = tok[a, at, :].astype(F32)
        inv = lax.rsqrt(jnp.mean(v * v, axis=-1, keepdims=True) + EPS)
        hid[a, at, :] = ((v * inv) * gain[...]).astype(BF16)
        return carry

    lax.fori_loop(0, BL * 4, norm, 0)

    ex_a = exchange_in(fm, moved, s_a, r_a, x, c, y, z)
    for h in range(2):
        for g in range(h, G, 2):
            cols = slice(g * GW, (g + 1) * GW)
            v = dot(fine[g], blocks(hid, cols)).astype(BF16)
            for a in range(BL):
                fm[a, :, cols] = v[:, a * NB : a * NB + NB]
        if h == 0:
            pl.semaphore_wait(bar, count)
            start_all(gz, NZ)
        else:
            recv_all(gz, NZ)
            for zz in range(NZ):
                wrow[4 * zz : 4 * zz + 4, :] = wz[zz].astype(F32)
            w[x, c, y] = wrow[...].astype(BF16)
            start_all(ga_y, NY)
            start_all(gb_x, NX)
        start_all(ex_a(h, 0, BL, GW * h, GW), NY * NZ)
    own_in(fm, moved, x, c, y, z)

    recv_all(ga_y, NY)
    start_all(ga_x, NX)
    recv_all(gb_x, NX)
    start_all(gb_y, NY)
    ga_c(0).start()
    gb_c(0).start()

    for h in range(2):
        ex_a(h, 0, BL, GW * h, GW).recv()
        to_rows(moved, tallm, h)
        coarse_mix(coarse[2 * y + h], tallm, tall2, h, 1)
        from_rows(tall2, back, h)
    ex_b = exchange_out(back, mixed, s_b, r_b, x, c, y, z)
    start_all(ex_b(0, 0, 2, 0, QW), NY * NZ)
    start_all(ex_b(1, 2, 2, 0, QW), NY * NZ)
    own_out(back, mixed, x, c, y, z)

    def gather_x(k, carry):
        ga_x(k).wait_recv()
        ga_c(k).start()
        gb_y(k).wait_recv()
        gb_c(k).start()
        return carry

    lax.fori_loop(1, NX, gather_x, 0)
    for k in range(NX):
        ga_c(k).wait_recv()
        gb_c(k).wait_recv()

    glm8[...] = jnp.zeros_like(glm8)
    ex_d = exchange_in(bm, xin, s_d, r_d, x, c, y, z)
    HALF = ROWS // 2

    def mlp(i, carry):
        rows = pl.ds(pl.multiple_of(i * HALF, HALF), HALF)
        ex_b(i, 2 * i, 2, 0, QW).recv()

        def pre(r, carry):
            a = 2 * i + r // 8
            at = pl.ds(pl.multiple_of((r % 8) * 16, 16), 16)
            to = pl.ds(pl.multiple_of(i * HALF + r * 16, 16), 16)
            v = tok[a, at, :].astype(F32) + mixed[a, at, :].astype(F32) * hid[a, at, :].astype(F32)
            inv = lax.rsqrt(jnp.mean(v * v, axis=-1, keepdims=True) + EPS)
            after[to, :] = v
            invs[to, :] = jnp.broadcast_to(inv, (16, 128))
            mlp_in[to, :] = ((v * inv) * gain2[...]).astype(BF16)
            return carry

        lax.fori_loop(0, HALF // 16, pre, 0)

        def hidden(n, carry):
            lane = pl.multiple_of(n * 256, 256)
            cols = pl.ds(lane, 256)
            cols2 = pl.ds(pl.multiple_of(FF + lane, 256), 256)
            cols3 = pl.ds(pl.multiple_of(2 * FF + lane, 256), 256)
            m = mlp_in[rows, :]
            gate = dot(m, w[:, :, :, :, cols].reshape(D, 256))
            up = dot(m, w[:, :, :, :, cols2].reshape(D, 256))
            ba = dot(cot[rows, :], w[:, :, :, :, cols3].reshape(D, 256)).astype(BF16).astype(F32)
            sq = jax.nn.sigmoid(gate)
            sg = gate * sq
            act[rows, cols] = (sg * up).astype(BF16)
            bboth[rows, cols] = (ba * up * (sq * (1.0 + gate * (1.0 - sq)))).astype(BF16)
            bboth[rows, cols2] = (ba * sg).astype(BF16)
            return carry

        lax.fori_loop(0, FF // 256, hidden, 0)

        def up_back(m, carry):
            cols = pl.ds(pl.multiple_of(m * 256, 256), 256)
            bmi[rows, cols] = dot(bboth[rows, :], w[m, :, :, :, : 2 * FF].reshape(256, 2 * FF), 1, 1)
            return carry

        lax.fori_loop(0, D // 256, up_back, 0)

        def post(r, total):
            a = 2 * i + r // 8
            at = pl.ds(pl.multiple_of((r % 8) * 16, 16), 16)
            to = pl.ds(pl.multiple_of(i * HALF + r * 16, 16), 16)
            inv = invs[to, 0:1]
            n2 = after[to, :] * inv
            v = bmi[to, :]
            prod = v * n2
            w2 = v * gain2[...]
            center = jnp.mean(w2 * n2, axis=-1, keepdims=True)
            ba = cot[to, :].astype(F32) + inv * (w2 - n2 * center)
            bmi[to, :] = ba
            bm[a, at, :] = (ba * hid[a, at, :].astype(F32)).astype(BF16)
            return total + prod[:8] + prod[8:]

        glm8[...] = lax.fori_loop(0, HALF // 16, post, glm8[...])

        @pl.when(i == 0)
        def _():
            start_all(ex_d(0, 0, 2, 0, QW), NY * NZ)

        return carry

    lax.fori_loop(0, 2, mlp, 0)
    for h in range(2):
        start_all(ex_d(1 + h, 2, 2, GW * h, GW), NY * NZ)
    own_in(bm, xin, x, c, y, z)

    def part(d, put):
        at = pl.ds(pl.multiple_of(d * 128, 128), 128)
        lhs = mlp_in[:, at]
        for n in range(4):
            cols = slice(512 * n, 512 * n + 512)
            put(cols, dot(lhs, bboth[:, cols], 0, 0))
        lhs = cot[:, at]
        for n in range(2):
            cols = slice(512 * n, 512 * n + 512)
            put(slice(2 * FF + 512 * n, 2 * FF + 512 * n + 512), dot(lhs, act[:, cols], 0, 0))

    def core_copy(k):
        xx = lax.rem(x + k, NX)
        return send(pbuf.at[xx, 1 - c], crecv.at[k], s_c.at[k], r_c.at[k], sib, seq)

    def xa_copy(k):
        xx = lax.rem(x + k, NX)
        return send(
            pbuf.at[xx, c, :, :, HA], xrecv.at[k - 1], s_x.at[0, k], r_x.at[0, k], 2 * xx + c, seq
        )

    def yb_copy(k):
        yy = lax.rem(y + k, NY)
        return send(
            pbuf.at[:, c, yy, :, HB], brecv.at[k - 1], s_y.at[0, k], r_y.at[0, k], dp, yy * NZ + z
        )

    def ya_copy(k):
        yy = lax.rem(y + k, NY)
        return send(
            ysend.at[yy], yrecv.at[k - 1], s_y.at[1, k], r_y.at[1, k], dp, yy * NZ + z
        )

    def xb_copy(k):
        xx = lax.rem(x + k, NX)
        return send(
            bsend.at[xx], bxrecv.at[k - 1], s_x.at[1, k], r_x.at[1, k], 2 * xx + c, seq
        )

    def z_copy(k):
        zz = lax.rem(z + k, NZ)
        return send(zbuf.at[zz], zrecv.at[k - 1], s_z.at[k], r_z.at[k], dp, y * NZ + zz)

    def first(i, carry):
        xx = lax.rem(x + i + 1, NX)

        def put(cols, v):
            n = cols.stop - cols.start
            pbuf[xx, 1 - c, :, :, cols] = v.astype(BF16).reshape(NY, 32, n)

        part(2 * xx + 1 - c, put)
        core_copy(lax.rem(i + 1, NX)).start()
        return carry

    lax.fori_loop(0, NX, first, 0)

    def second(i, carry):
        k = lax.rem(i + 1, NX)
        xx = lax.rem(x + k, NX)
        core_copy(k).wait_recv()

        def put(cols, v):
            n = cols.stop - cols.start
            v = v.reshape(NY, 32, n) + crecv[k, :, :, cols].astype(F32)
            pbuf[xx, c, :, :, cols] = v.astype(BF16)

        part(2 * xx + c, put)

        @pl.when(k != 0)
        def _():
            xa_copy(k).start()

        return carry

    lax.fori_loop(0, NX, second, 0)
    start_all(yb_copy, NY)

    def weights_second():
        recv_all(xa_copy, NX)
        recv_all(yb_copy, NY)

        def add(yy, carry):
            for q in range(2):
                at = slice(16 * q, 16 * q + 16)
                v = pbuf[x, c, yy, at, HA].astype(F32)
                for k in range(NX - 1):
                    v = v + xrecv[k, yy, at, :].astype(F32)
                acc[yy, at, :] = v
                ysend[yy, at, :] = v.astype(BF16)
                v = pbuf[yy, c, y, at, HB].astype(F32)
                for k in range(NY - 1):
                    v = v + brecv[k, yy, at, :].astype(F32)
                accb[yy, at, :] = v
                bsend[yy, at, :] = v.astype(BF16)
            return carry

        lax.fori_loop(0, NX, add, 0)
        start_all(ya_copy, NY)
        start_all(xb_copy, NX)

    def weights_third():
        recv_all(ya_copy, NY)
        recv_all(xb_copy, NX)
        for q in range(4):
            at = slice(8 * q, 8 * q + 8)
            va = acc[y, at, :]
            for k in range(NY - 1):
                va = va + yrecv[k, at, :].astype(F32)
            vb = accb[x, at, :]
            for k in range(NX - 1):
                vb = vb + bxrecv[k, at, :].astype(F32)
            zbuf[2 * q, :, HA] = va[:4].astype(BF16)
            zbuf[2 * q + 1, :, HA] = va[4:].astype(BF16)
            zbuf[2 * q, :, HB] = vb[:4].astype(BF16)
            zbuf[2 * q + 1, :, HB] = vb[4:].astype(BF16)
        start_all(z_copy, NZ)

    ex_d(0, 0, 2, 0, QW).recv()
    ex_e = exchange_out(xout, bfine, s_e, r_e, x, c, y, z)
    for h in range(2):
        ex_d(1 + h, 2, 2, GW * h, GW).recv()
        to_rows(xin, tall, h)
        coarse_mix(coarse[2 * y + h], tall, tall2, h, 0)
        from_rows(tall2, xout, h)
        start_all(ex_e(h, 0, BL, GW * h, GW), NY * NZ)
    own_out(xout, bfine, x, c, y, z)

    for d in range(G):
        sc.v[d] = jnp.zeros((NC, NC), F32)
    for h in range(2):
        total = jnp.zeros((NC, NC), F32)
        for b in range(0, BW, 4):
            total = total + dot(columns(tall, h, b, 4), columns(tallm, h, b, 4), 1, 1)
        sc.v[2 * y + h] = total
    sc.start_a()

    sc.start_b()

    def project(m, carry):
        cols = pl.ds(pl.multiple_of(m * 256, 256), 256)
        v = dot(act[...], w[m, :, :, :, 2 * FF :].reshape(256, FF), 1, 1)
        layer[:, cols] = (after[:, cols] + v).astype(BF16)
        return carry

    lax.fori_loop(0, D // 256, project, 0)
    sc.start_c()

    weights_second()

    def fine_terms(h):
        for g in range(h, G, 2):
            cols = slice(g * GW, (g + 1) * GW)
            sf.v[g] = dot(blocks(bfine, cols), blocks(hid, cols), 1, 1)

    def back_hidden(h):
        for g in range(h, G, 2):
            cols = slice(g * GW, (g + 1) * GW)
            v = dot(fine[g], blocks(bfine, cols), 0, 0)
            for a in range(BL):
                bhid[a, :, cols] = (
                    bmi[a * NB : a * NB + NB, cols] * mixed[a, :, cols].astype(F32)
                    + v[:, a * NB : a * NB + NB]
                )

    ex_e(0, 0, BL, 0, GW).recv()
    fine_terms(0)
    back_hidden(0)
    ex_e(1, 0, BL, GW, GW).recv()
    fine_terms(1)
    sf.start_a()
    back_hidden(1)

    def sums(i, total):
        a = i // 8
        at = pl.ds(pl.multiple_of((i % 8) * 16, 16), 16)
        v = tok[a, at, :].astype(F32)
        inv = lax.rsqrt(jnp.mean(v * v, axis=-1, keepdims=True) + EPS)
        prod = bhid[a, at, :] * (v * inv)
        return total + prod[:8] + prod[8:]

    gm = lax.fori_loop(0, BL * 8, sums, jnp.zeros((8, D), F32))
    gm = jnp.sum(gm, axis=0, keepdims=True)
    gl = jnp.sum(glm8[...], axis=0, keepdims=True)
    for d in range(G):
        gloc[d, 0:1, :] = gm[:, d * GW : (d + 1) * GW]
        gloc[d, 1:2, :] = gl[:, d * GW : (d + 1) * GW]
        gloc[d, 2:, :] = jnp.zeros((6, GW), F32)
    sf.start_gain()
    sf.start_b()
    weights_third()

    def last(i, carry):
        a = i // 8
        at = pl.ds(pl.multiple_of((i % 8) * 16, 16), 16)
        to = pl.ds(pl.multiple_of(i * 16, 16), 16)
        v = tok[a, at, :].astype(F32)
        inv = lax.rsqrt(jnp.mean(v * v, axis=-1, keepdims=True) + EPS)
        normed = v * inv
        w1 = bhid[a, at, :] * gain[...]
        center = jnp.mean(w1 * normed, axis=-1, keepdims=True)
        gin[a, at, :] = (bmi[to, :] + inv * (w1 - normed * center)).astype(BF16)
        return carry

    lax.fori_loop(0, BL * 8, last, 0)
    sf.start_c()
    sc.start_d()
    sf.start_d()
    recv_all(z_copy, NZ)
    v = zbuf[z].astype(F32)
    for k in range(NZ - 1):
        v = v + zrecv[k].astype(F32)
    wsum[...] = v

    sent_all(gz, NZ)
    for copy in (ga_y, ga_x, gb_x, gb_y, xa_copy, yb_copy, ya_copy, xb_copy):
        sent_all(copy, 4)
    for k in range(NX):
        ga_c(k).wait_send()
        gb_c(k).wait_send()
        core_copy(k).wait_send()
    sent_all(z_copy, NZ)
    for h in range(2):
        ex_a(h, 0, BL, GW * h, GW).sent()
        ex_b(h, 2 * h, 2, 0, QW).sent()
        ex_d(1 + h, 2, 2, GW * h, GW).sent()
        ex_e(h, 0, BL, GW * h, GW).sent()
    ex_d(0, 0, 2, 0, QW).sent()
    sc.finish()
    sf.finish()


def finish_kernel(
    gin, layer, wsum, fevery, cevery, gevery,
    ogin, olayer, ogu, odn, ofine, ocoarse, omix, omlp,
):
    olayer[0] = layer[...]
    ogin[0] = gin[...].reshape(ROWS, D)
    scale = 1.0 / math.sqrt(8 * NC * NB)
    ogu[...] = wsum[:, : 2 * FF] * scale
    odn[...] = wsum[:, 2 * FF :] * scale
    lower = lax.broadcasted_iota(jnp.int32, (128, 128), 0) >= lax.broadcasted_iota(
        jnp.int32, (128, 128), 1
    )
    small = 1.0 / math.sqrt(8 * NC * GW)
    for d in range(G):
        ofine[d] = jnp.where(lower, fevery[d].astype(F32) * small, 0.0)
        ocoarse[d] = jnp.where(lower, cevery[d].astype(F32) * small, 0.0)
        omix[:, d * GW : (d + 1) * GW] = gevery[d, 4:5, :] * scale
        omlp[:, d * GW : (d + 1) * GW] = gevery[d, 5:6, :] * scale


def vmem(n):
    return [pl.BlockSpec(memory_space=pltpu.VMEM)] * n


def on_device(tokens, cotangent, gain_mix, gain_mlp, fine, coarse, w_gate_up, w_down):
    S = jax.ShapeDtypeStruct
    V = pltpu.VMEM
    parts = pl.pallas_call(
        layer_kernel,
        name="layer",
        out_shape=(
            S((BL, NB, D), BF16),
            S((ROWS, D), BF16),
            S((4, WC), F32),
            S((G, 128, 128), BF16),
            S((G, 128, 128), BF16),
            S((G, 8, 128), F32),
        ),
        in_specs=vmem(8),
        out_specs=tuple(vmem(6)),
        scratch_shapes=[
            V((BL, NB, D), BF16),
            V((BL, NB, D), BF16),
            V((NC, BW, QW), BF16),
            V((NC, BW, QW), BF16),
            V((BL, NB, D), BF16),
            V((BL, NB, D), BF16),
            V((NC, BW, QW), BF16),
            V((NC, BW, QW), BF16),
            V((BL, NB, D), BF16),
            V((BL, NB, D), F32),
            V((2, NC * BW, GW), F32),
            V((2, NC * BW, GW), F32),
            V((2, NC * BW, GW), F32),
            V((NZ, 4, WC), BF16),
            V((32, WC), F32),
            V((NX, 2, NY, 32, WC), BF16),
            V((ROWS, D), F32),
            V((ROWS, 128), F32),
            V((ROWS, D), BF16),
            V((ROWS, FF), BF16),
            V((ROWS, 2 * FF), BF16),
            V((ROWS, D), F32),
            V((8, D), F32),
            V((NX, 2, NY, 32, WC), BF16),
            V((NX, NY, 32, WC), BF16),
            V((3, NY, 32, WC // 2), BF16),
            V((3, NX, 32, WC // 2), BF16),
            V((NY, 32, WC // 2), F32),
            V((NX, 32, WC // 2), F32),
            V((NY, 32, WC // 2), BF16),
            V((NX, 32, WC // 2), BF16),
            V((3, 32, WC // 2), BF16),
            V((3, 32, WC // 2), BF16),
            V((8, 4, WC), BF16),
            V((7, 4, WC), BF16),
            dma(2), dma(2), dma(2), dma(2),
            dma(3), dma(3), dma(2), dma(2),
            dma(7, 8), dma(7, 8),
            dma(4), dma(4), dma(2, 4), dma(2, 4), dma(2, 4), dma(2, 4), dma(8), dma(8),
            V((8, 8, 128), F32), V((8, 8, 128), F32), dma(2), dma(2),
            *small_scratch(), *small_scratch(),
        ],
        compiler_params=pltpu.CompilerParams(
            collective_id=0, has_side_effects=True, vmem_limit_bytes=63 * 1024 * 1024
        ),
    )(
        tokens.reshape(BL, NB, D), cotangent.reshape(ROWS, D),
        gain_mix.reshape(1, D), gain_mlp.reshape(1, D), fine, coarse, w_gate_up, w_down,
    )
    gin, layer, ogu, odn, ofine, ocoarse, omix, omlp = pl.pallas_call(
        finish_kernel,
        name="finish",
        out_shape=(
            S((1, ROWS, D), BF16),
            S((1, ROWS, D), BF16),
            S((4, 2 * FF), F32),
            S((4, FF), F32),
            S((G, NB, NB), F32),
            S((G, NC, NC), F32),
            S((1, D), F32),
            S((1, D), F32),
        ),
        in_specs=vmem(6),
        out_specs=tuple(vmem(8)),
    )(*parts)
    return (layer, gin, ogu, odn, ofine, ocoarse, omix.reshape(D), omlp.reshape(D))


def solution(mesh):
    rows = P("dp", "seq", None)
    weights = P(("dp", "seq"), None)
    return jax.shard_map(
        on_device,
        mesh=mesh,
        in_specs=(rows, rows, P(), P(), P(), P(), weights, weights),
        out_specs=(rows, rows, weights, weights, P(), P(), P(), P()),
        check_vma=False,
    )
```

```python
import math

import jax
import jax.numpy as jnp
from jax import lax
from jax.experimental import pallas as pl
from jax.experimental.pallas import tpu as pltpu
from jax.sharding import PartitionSpec as P

D = 1024
FF = 1024
NB = 128
NC = 128
GW = 128
G = 8
NX, NY, NZ = 4, 4, 8
BL = 4
QW = 256
BW = 16
ROWS = BL * NB
WC = 3 * FF
EPS = 1e-05
MESH = pl.DeviceIdType.MESH
F32 = jnp.float32
BF16 = jnp.bfloat16


def place():
    dp = lax.axis_index("dp")
    seq = lax.axis_index("seq")
    return lax.div(dp, 2), lax.rem(dp, 2), lax.div(seq, NZ), lax.rem(seq, NZ)


def shifted(y, z, k):
    return lax.rem(y + lax.div(k, NZ), NY), lax.rem(z + lax.rem(k, NZ), NZ)


def send(src, dst, ssem, rsem, dp, seq):
    return pltpu.make_async_remote_copy(
        src_ref=src,
        dst_ref=dst,
        send_sem=ssem,
        recv_sem=rsem,
        device_id=(dp, seq),
        device_id_type=MESH,
    )


def greet(x, c, y, z):
    bar = pltpu.get_barrier_semaphore()

    def one(dp, seq):
        pl.semaphore_signal(bar, inc=1, device_id=(dp, seq), device_id_type=MESH)

    def plane(k, carry):
        ty, tz = shifted(y, z, k)
        one(2 * x + c, ty * NZ + tz)
        return carry

    lax.fori_loop(1, NY * NZ, plane, 0)
    for k in range(1, 2 * NX):
        one((2 * x + c + k) % (2 * NX), y * NZ + z)
    return bar, NY * NZ - 1 + 2 * NX - 1


def dot(a, b, ca=1, cb=0):
    return lax.dot_general(a, b, (((ca,), (cb,)), ((), ())), preferred_element_type=F32)


def exchange_in(src, dst, ssem, rsem, x, c, y, z):
    me = y * NZ + z

    def part(slot, first, count, lane, width):
        def copy(k):
            ty, tz = shifted(y, z, k)
            return send(
                src.at[
                    pl.ds(first, count),
                    pl.ds(pl.multiple_of(BW * tz, BW), BW),
                    pl.ds(pl.multiple_of(QW * ty + lane, GW), width),
                ],
                dst.at[pl.ds(BL * me + first, count), :, pl.ds(lane, width)],
                ssem.at[slot],
                rsem.at[slot],
                2 * x + c,
                ty * NZ + tz,
            )

        seen = dst.at[pl.ds(0, count * (NY * NZ - 1)), :, pl.ds(lane, width)]
        copy.recv = lambda: bulk(seen, rsem.at[slot])
        copy.sent = lambda: bulk(seen, ssem.at[slot])
        return copy

    return part


def exchange_out(src, dst, ssem, rsem, x, c, y, z):
    def part(slot, first, count, lane, width):
        def copy(k):
            ty, tz = shifted(y, z, k)
            to = ty * NZ + tz
            return send(
                src.at[pl.ds(BL * to + first, count), :, pl.ds(lane, width)],
                dst.at[
                    pl.ds(first, count),
                    pl.ds(pl.multiple_of(BW * z, BW), BW),
                    pl.ds(pl.multiple_of(QW * y + lane, GW), width),
                ],
                ssem.at[slot],
                rsem.at[slot],
                2 * x + c,
                to,
            )

        seen = src.at[pl.ds(0, count * (NY * NZ - 1)), :, pl.ds(lane, width)]
        copy.recv = lambda: bulk(seen, rsem.at[slot])
        copy.sent = lambda: bulk(seen, ssem.at[slot])
        return copy

    return part


def bulk(ref, sem):
    pltpu.make_async_copy(ref, ref, sem).wait()


def start_all(copy, n):
    def body(k, carry):
        copy(k).start()
        return carry

    lax.fori_loop(1, n, body, 0)


def recv_all(copy, n):
    def body(k, carry):
        copy(k).wait_recv()
        return carry

    lax.fori_loop(1, n, body, 0)


def sent_all(copy, n):
    def body(k, carry):
        copy(k).wait_send()
        return carry

    lax.fori_loop(1, n, body, 0)


def to_rows(src, tall, h):
    def body(i, carry):
        v = src[pl.ds(8 * i, 8), :, GW * h : GW * h + GW].reshape(8 * BW, GW).astype(F32)
        tall[h, pl.ds(pl.multiple_of(8 * BW * i, 8 * BW), 8 * BW), :] = v
        return carry

    lax.fori_loop(0, NC // 8, body, 0)


def from_rows(tall, dst, h):
    def body(i, carry):
        v = tall[h, pl.ds(pl.multiple_of(8 * BW * i, 8 * BW), 8 * BW), :].astype(BF16)
        dst[pl.ds(8 * i, 8), :, GW * h : GW * h + GW] = v.reshape(8, BW, GW)
        return carry

    lax.fori_loop(0, NC // 8, body, 0)


def columns(tall, h, first, count):
    at = [tall[h, pl.ds(b, NC, stride=BW), :].astype(BF16) for b in range(first, first + count)]
    return jnp.concatenate(at, axis=1)


def coarse_mix(factor, tall, out, h, side):
    for b in range(0, BW, 4):
        v = dot(factor, columns(tall, h, b, 4), side, 0)
        for n in range(4):
            out[h, pl.ds(b + n, NC, stride=BW), :] = v[:, n * GW : n * GW + GW]


def own_in(src, dst, x, c, y, z):
    dst[pl.ds(BL * (y * NZ + z), BL)] = src[
        :, pl.ds(pl.multiple_of(BW * z, BW), BW), pl.ds(pl.multiple_of(QW * y, QW), QW)
    ]


def own_out(src, dst, x, c, y, z):
    dst[:, pl.ds(pl.multiple_of(BW * z, BW), BW), pl.ds(pl.multiple_of(QW * y, QW), QW)] = src[
        pl.ds(BL * (y * NZ + z), BL)
    ]


class SmallSum:
    def __init__(self, refs, sems, gain, x, c, y, z):
        self.v, self.vs, self.vr, self.pieces, self.pr, self.cg, self.full, self.every = refs[:8]
        self.ss, self.rs = sems
        self.gain = gain
        self.dp, self.y, self.z = 2 * x + c, y, z
        self.seq = y * NZ + z

    def plane(self, k):
        ty, tz = shifted(self.y, self.z, k)
        return ty * NZ + tz

    def a(self, k):
        to = lax.rem(self.dp + k, 8)
        return send(self.vs.at[to], self.vr.at[k], self.ss.at[0], self.rs.at[0], to, self.seq)

    def ga(self, k):
        to = lax.rem(self.dp + k, 8)
        loc, rec, _, _, gs, gr = self.gain
        return send(loc.at[to], rec.at[k], gs.at[0], gr.at[0], to, self.seq)

    def b(self, k):
        to = self.plane(k)
        return send(
            self.pieces.at[to], self.pr.at[k], self.ss.at[1], self.rs.at[1], self.dp, to
        )

    def c(self, k):
        return send(
            self.cg.at[self.seq], self.cg.at[self.seq],
            self.ss.at[2], self.rs.at[2], self.dp, self.plane(k),
        )

    def d(self, k):
        to = lax.rem(self.dp + k, 8)
        return send(
            self.every.at[self.dp], self.every.at[self.dp],
            self.ss.at[3], self.rs.at[3], to, self.seq,
        )

    def gd(self, k):
        to = lax.rem(self.dp + k, 8)
        _, _, _, ge, gs, gr = self.gain
        return send(ge.at[self.dp], ge.at[self.dp], gs.at[1], gr.at[1], to, self.seq)

    def start_a(self):
        for d in range(G):
            self.vs[d] = self.v[d].astype(BF16)
        start_all(self.a, 8)

    def start_gain(self):
        start_all(self.ga, 8)

    def start_b(self):
        bulk(self.vr.at[pl.ds(1, 7)], self.rs.at[0])
        s = self.v[self.dp]
        for k in range(1, 8):
            s = s + self.vr[k].astype(F32)
        if self.gain is not None:
            loc, rec, _, _, gs, gr = self.gain
            bulk(rec.at[pl.ds(1, 7)], gr.at[0])
            t = loc[self.dp]
            for k in range(1, 8):
                t = t + rec[k]
            t = t[:4]
        else:
            t = jnp.zeros((4, 128), F32)
        for j in range(NY * NZ):
            self.pieces[j, :4, :] = s[4 * j : 4 * j + 4]
            self.pieces[j, 4:, :] = t
        start_all(self.b, NY * NZ)

    def start_c(self):
        bulk(self.pr.at[pl.ds(1, NY * NZ - 1)], self.rs.at[1])
        s = self.pieces[self.seq]
        for k in range(1, NY * NZ):
            s = s + self.pr[k]
        self.cg[self.seq] = s
        start_all(self.c, NY * NZ)

    def start_d(self):
        bulk(self.cg.at[pl.ds(0, NY * NZ - 1)], self.rs.at[2])
        if self.gain is not None:
            self.gain[3][self.dp] = self.cg[0]
            start_all(self.gd, 8)
        for j in range(NY * NZ):
            self.full[4 * j : 4 * j + 4, :] = self.cg[j, :4, :]
        self.every[self.dp] = self.full[...].astype(BF16)
        start_all(self.d, 8)

    def finish(self):
        bulk(self.every.at[pl.ds(0, 7)], self.rs.at[3])
        bulk(self.vs.at[pl.ds(0, 7)], self.ss.at[0])
        bulk(self.pieces.at[pl.ds(0, NY * NZ - 1)], self.ss.at[1])
        bulk(self.cg.at[pl.ds(0, NY * NZ - 1)], self.ss.at[2])
        bulk(self.every.at[pl.ds(0, 7)], self.ss.at[3])
        if self.gain is not None:
            loc, _, _, ge, gs, gr = self.gain
            bulk(ge.at[pl.ds(0, 7)], gr.at[1])
            bulk(loc.at[pl.ds(0, 7)], gs.at[0])
            bulk(ge.at[pl.ds(0, 7)], gs.at[1])


def small_scratch():
    V = pltpu.VMEM
    return [
        V((8, 128, 128), F32),
        V((8, 128, 128), BF16),
        V((8, 128, 128), BF16),
        V((32, 8, 128), F32),
        V((32, 8, 128), F32),
        V((32, 8, 128), F32),
        V((128, 128), F32),
        dma(4),
        dma(4),
    ]


def dma(*shape):
    return pltpu.SemaphoreType.DMA(shape)


def blocks(ref, cols):
    return jnp.concatenate([ref[a, :, cols] for a in range(BL)], axis=1)


def layer_kernel(
    tok, cot, gain, gain2, fine, coarse, wgu, wdn,
    gin, layer, wsum, fevery, cevery, gevery,
    hid, fm, moved, back, mixed, bm, xin, xout, bfine, bhid, tall, tall2, tallm,
    wz, wrow, w,
    after, invs, mlp_in, act, bboth, bmi, glm8,
    pbuf, crecv, xrecv, brecv, acc, accb, ysend, bsend, yrecv, bxrecv, zbuf, zrecv,
    s_a, r_a, s_b, r_b, s_d, r_d, s_e, r_e,
    s_g, r_g, s_x0, r_x0, s_y0, r_y0, s_c, r_c, s_x, r_x, s_y, r_y, s_z, r_z,
    gloc, grec, gs, gr,
    *small,
):
    x, c, y, z = place()
    dp = 2 * x + c
    seq = y * NZ + z
    sib = 2 * x + 1 - c
    bar, count = greet(x, c, y, z)
    sf = SmallSum((*small[:7], fevery), small[7:9], (gloc, grec, None, gevery, gs, gr), x, c, y, z)
    sc = SmallSum((*small[9:16], cevery), small[16:18], None, x, c, y, z)

    wz[pl.ds(z, 1), :, : 2 * FF] = wgu[...].reshape(1, 4, 2 * FF)
    wz[pl.ds(z, 1), :, 2 * FF :] = wdn[...].reshape(1, 4, FF)
    HA = slice(0, WC // 2)
    HB = slice(WC // 2, WC)

    def gz(k):
        tz = (z + k) % NZ
        return send(wz.at[z], wz.at[z], s_g.at[0, k], r_g.at[0, k], dp, y * NZ + tz)

    def ga_y(k):
        at = w.at[x, c, y, :, HA]
        return send(at, at, s_g.at[1, k], r_g.at[1, k], dp, ((y + k) % NY) * NZ + z)

    def ga_x(k, j=0):
        at = w.at[x, c, lax.rem(y + NY - j, NY), :, HA]
        return send(at, at, s_x0.at[j, k], r_x0.at[j, k], 2 * lax.rem(x + k, NX) + c, seq)

    def ga_c(k):
        at = w.at[(x + NX - k) % NX, c, :, :, HA]
        return send(at, at, s_g.at[3, k], r_g.at[3, k], sib, seq)

    def gb_x(k):
        at = w.at[x, c, y, :, HB]
        return send(at, at, s_g.at[4, k], r_g.at[4, k], 2 * ((x + k) % NX) + c, seq)

    def gb_y(k, j=0):
        at = w.at[lax.rem(x + NX - j, NX), c, y, :, HB]
        return send(at, at, s_y0.at[j, k], r_y0.at[j, k], dp, lax.rem(y + k, NY) * NZ + z)

    def gb_c(k):
        at = w.at[:, c, (y + NY - k) % NY, :, HB]
        return send(at, at, s_g.at[6, k], r_g.at[6, k], sib, seq)

    def norm(i, carry):
        a = i // 4
        at = pl.ds(pl.multiple_of((i % 4) * 32, 32), 32)
        v = tok[a, at, :].astype(F32)
        inv = lax.rsqrt(jnp.mean(v * v, axis=-1, keepdims=True) + EPS)
        hid[a, at, :] = ((v * inv) * gain[...]).astype(BF16)
        return carry

    lax.fori_loop(0, BL * 4, norm, 0)

    ex_a = exchange_in(fm, moved, s_a, r_a, x, c, y, z)
    for h in range(2):
        for g in range(h, G, 2):
            cols = slice(g * GW, (g + 1) * GW)
            v = dot(fine[g], blocks(hid, cols)).astype(BF16)
            for a in range(BL):
                fm[a, :, cols] = v[:, a * NB : a * NB + NB]
        if h == 0:
            pl.semaphore_wait(bar, count)
            start_all(gz, NZ)
        else:
            recv_all(gz, NZ)
            for zz in range(NZ):
                wrow[4 * zz : 4 * zz + 4, :] = wz[zz].astype(F32)
            w[x, c, y] = wrow[...].astype(BF16)
            start_all(ga_y, NY)
            start_all(gb_x, NX)
            start_all(ga_x, NX)
            start_all(gb_y, NY)
        start_all(ex_a(h, 0, BL, GW * h, GW), NY * NZ)
    own_in(fm, moved, x, c, y, z)

    for j in (1, 3, 2):
        ga_y(j).wait_recv()
        for k in (1, 3, 2):
            ga_x(k, j).start()
        gb_x(j).wait_recv()
        for k in (1, 3, 2):
            gb_y(k, j).start()
    ga_c(0).start()
    gb_c(0).start()

    for h in range(2):
        ex_a(h, 0, BL, GW * h, GW).recv()
        to_rows(moved, tallm, h)
        coarse_mix(coarse[2 * y + h], tallm, tall2, h, 1)
        from_rows(tall2, back, h)
    ex_b = exchange_out(back, mixed, s_b, r_b, x, c, y, z)
    start_all(ex_b(0, 0, 2, 0, QW), NY * NZ)
    start_all(ex_b(1, 2, 2, 0, QW), NY * NZ)
    own_out(back, mixed, x, c, y, z)

    for k in (1, 3, 2):
        for j in range(NY):
            ga_x(k, j).wait_recv()
        ga_c(k).start()
        for j in range(NX):
            gb_y(k, j).wait_recv()
        gb_c(k).start()
    for k in range(NX):
        ga_c(k).wait_recv()
        gb_c(k).wait_recv()

    glm8[...] = jnp.zeros_like(glm8)
    ex_d = exchange_in(bm, xin, s_d, r_d, x, c, y, z)
    HALF = ROWS // 2

    def mlp(i, carry):
        rows = pl.ds(pl.multiple_of(i * HALF, HALF), HALF)
        ex_b(i, 2 * i, 2, 0, QW).recv()

        def pre(r, carry):
            a = 2 * i + r // 8
            at = pl.ds(pl.multiple_of((r % 8) * 16, 16), 16)
            to = pl.ds(pl.multiple_of(i * HALF + r * 16, 16), 16)
            v = tok[a, at, :].astype(F32) + mixed[a, at, :].astype(F32) * hid[a, at, :].astype(F32)
            inv = lax.rsqrt(jnp.mean(v * v, axis=-1, keepdims=True) + EPS)
            after[to, :] = v
            invs[to, :] = jnp.broadcast_to(inv, (16, 128))
            mlp_in[to, :] = ((v * inv) * gain2[...]).astype(BF16)
            return carry

        lax.fori_loop(0, HALF // 16, pre, 0)

        def hidden(n, carry):
            lane = pl.multiple_of(n * 256, 256)
            cols = pl.ds(lane, 256)
            cols2 = pl.ds(pl.multiple_of(FF + lane, 256), 256)
            cols3 = pl.ds(pl.multiple_of(2 * FF + lane, 256), 256)
            m = mlp_in[rows, :]
            gate = dot(m, w[:, :, :, :, cols].reshape(D, 256))
            up = dot(m, w[:, :, :, :, cols2].reshape(D, 256))
            ba = dot(cot[rows, :], w[:, :, :, :, cols3].reshape(D, 256)).astype(BF16).astype(F32)
            sq = jax.nn.sigmoid(gate)
            sg = gate * sq
            act[rows, cols] = (sg * up).astype(BF16)
            bboth[rows, cols] = (ba * up * (sq * (1.0 + gate * (1.0 - sq)))).astype(BF16)
            bboth[rows, cols2] = (ba * sg).astype(BF16)
            return carry

        lax.fori_loop(0, FF // 256, hidden, 0)

        def up_back(m, carry):
            cols = pl.ds(pl.multiple_of(m * 256, 256), 256)
            bmi[rows, cols] = dot(bboth[rows, :], w[m, :, :, :, : 2 * FF].reshape(256, 2 * FF), 1, 1)
            return carry

        lax.fori_loop(0, D // 256, up_back, 0)

        def post(r, total):
            a = 2 * i + r // 8
            at = pl.ds(pl.multiple_of((r % 8) * 16, 16), 16)
            to = pl.ds(pl.multiple_of(i * HALF + r * 16, 16), 16)
            inv = invs[to, 0:1]
            n2 = after[to, :] * inv
            v = bmi[to, :]
            prod = v * n2
            w2 = v * gain2[...]
            center = jnp.mean(w2 * n2, axis=-1, keepdims=True)
            ba = cot[to, :].astype(F32) + inv * (w2 - n2 * center)
            bmi[to, :] = ba
            bm[a, at, :] = (ba * hid[a, at, :].astype(F32)).astype(BF16)
            return total + prod[:8] + prod[8:]

        glm8[...] = lax.fori_loop(0, HALF // 16, post, glm8[...])

        @pl.when(i == 0)
        def _():
            start_all(ex_d(0, 0, 2, 0, QW), NY * NZ)

        return carry

    lax.fori_loop(0, 2, mlp, 0)
    for h in range(2):
        start_all(ex_d(1 + h, 2, 2, GW * h, GW), NY * NZ)
    own_in(bm, xin, x, c, y, z)

    def part(d, put):
        at = pl.ds(pl.multiple_of(d * 128, 128), 128)
        lhs = mlp_in[:, at]
        for n in range(4):
            cols = slice(512 * n, 512 * n + 512)
            put(cols, dot(lhs, bboth[:, cols], 0, 0))
        lhs = cot[:, at]
        for n in range(2):
            cols = slice(512 * n, 512 * n + 512)
            put(slice(2 * FF + 512 * n, 2 * FF + 512 * n + 512), dot(lhs, act[:, cols], 0, 0))

    def core_copy(k):
        xx = lax.rem(x + k, NX)
        return send(pbuf.at[xx, 1 - c], crecv.at[k], s_c.at[k], r_c.at[k], sib, seq)

    def xa_copy(k):
        xx = lax.rem(x + k, NX)
        return send(
            pbuf.at[xx, c, :, :, HA], xrecv.at[k - 1], s_x.at[0, k], r_x.at[0, k], 2 * xx + c, seq
        )

    def yb_copy(k):
        yy = lax.rem(y + k, NY)
        return send(
            pbuf.at[:, c, yy, :, HB], brecv.at[k - 1], s_y.at[0, k], r_y.at[0, k], dp, yy * NZ + z
        )

    def ya_copy(k):
        yy = lax.rem(y + k, NY)
        return send(
            ysend.at[yy], yrecv.at[k - 1], s_y.at[1, k], r_y.at[1, k], dp, yy * NZ + z
        )

    def xb_copy(k):
        xx = lax.rem(x + k, NX)
        return send(
            bsend.at[xx], bxrecv.at[k - 1], s_x.at[1, k], r_x.at[1, k], 2 * xx + c, seq
        )

    def z_copy(k):
        zz = lax.rem(z + k, NZ)
        return send(zbuf.at[zz], zrecv.at[k - 1], s_z.at[k], r_z.at[k], dp, y * NZ + zz)

    def first(i, carry):
        xx = lax.rem(x + i + 1, NX)

        def put(cols, v):
            n = cols.stop - cols.start
            pbuf[xx, 1 - c, :, :, cols] = v.astype(BF16).reshape(NY, 32, n)

        part(2 * xx + 1 - c, put)
        core_copy(lax.rem(i + 1, NX)).start()
        return carry

    lax.fori_loop(0, NX, first, 0)

    def second(i, carry):
        k = lax.rem(i + 1, NX)
        xx = lax.rem(x + k, NX)
        core_copy(k).wait_recv()

        def put(cols, v):
            n = cols.stop - cols.start
            v = v.reshape(NY, 32, n) + crecv[k, :, :, cols].astype(F32)
            pbuf[xx, c, :, :, cols] = v.astype(BF16)

        part(2 * xx + c, put)

        @pl.when(k != 0)
        def _():
            xa_copy(k).start()

        return carry

    lax.fori_loop(0, NX, second, 0)
    start_all(yb_copy, NY)

    def weights_second():
        recv_all(xa_copy, NX)
        recv_all(yb_copy, NY)

        def add(yy, carry):
            for q in range(2):
                at = slice(16 * q, 16 * q + 16)
                v = pbuf[x, c, yy, at, HA].astype(F32)
                for k in range(NX - 1):
                    v = v + xrecv[k, yy, at, :].astype(F32)
                acc[yy, at, :] = v
                ysend[yy, at, :] = v.astype(BF16)
                v = pbuf[yy, c, y, at, HB].astype(F32)
                for k in range(NY - 1):
                    v = v + brecv[k, yy, at, :].astype(F32)
                accb[yy, at, :] = v
                bsend[yy, at, :] = v.astype(BF16)
            return carry

        lax.fori_loop(0, NX, add, 0)
        start_all(ya_copy, NY)
        start_all(xb_copy, NX)

    def weights_third():
        recv_all(ya_copy, NY)
        recv_all(xb_copy, NX)
        for q in range(4):
            at = slice(8 * q, 8 * q + 8)
            va = acc[y, at, :]
            for k in range(NY - 1):
                va = va + yrecv[k, at, :].astype(F32)
            vb = accb[x, at, :]
            for k in range(NX - 1):
                vb = vb + bxrecv[k, at, :].astype(F32)
            zbuf[2 * q, :, HA] = va[:4].astype(BF16)
            zbuf[2 * q + 1, :, HA] = va[4:].astype(BF16)
            zbuf[2 * q, :, HB] = vb[:4].astype(BF16)
            zbuf[2 * q + 1, :, HB] = vb[4:].astype(BF16)
        start_all(z_copy, NZ)

    ex_d(0, 0, 2, 0, QW).recv()
    ex_e = exchange_out(xout, bfine, s_e, r_e, x, c, y, z)
    for h in range(2):
        ex_d(1 + h, 2, 2, GW * h, GW).recv()
        to_rows(xin, tall, h)
        coarse_mix(coarse[2 * y + h], tall, tall2, h, 0)
        from_rows(tall2, xout, h)
        start_all(ex_e(h, 0, BL, GW * h, GW), NY * NZ)
    own_out(xout, bfine, x, c, y, z)

    for d in range(G):
        sc.v[d] = jnp.zeros((NC, NC), F32)
    for h in range(2):
        total = jnp.zeros((NC, NC), F32)
        for b in range(0, BW, 4):
            total = total + dot(columns(tall, h, b, 4), columns(tallm, h, b, 4), 1, 1)
        sc.v[2 * y + h] = total
    sc.start_a()

    sc.start_b()

    def project(m, carry):
        cols = pl.ds(pl.multiple_of(m * 256, 256), 256)
        v = dot(act[...], w[m, :, :, :, 2 * FF :].reshape(256, FF), 1, 1)
        layer[:, cols] = (after[:, cols] + v).astype(BF16)
        return carry

    lax.fori_loop(0, D // 256, project, 0)
    sc.start_c()

    weights_second()

    def fine_terms(h):
        for g in range(h, G, 2):
            cols = slice(g * GW, (g + 1) * GW)
            sf.v[g] = dot(blocks(bfine, cols), blocks(hid, cols), 1, 1)

    def back_hidden(h):
        for g in range(h, G, 2):
            cols = slice(g * GW, (g + 1) * GW)
            v = dot(fine[g], blocks(bfine, cols), 0, 0)
            for a in range(BL):
                bhid[a, :, cols] = (
                    bmi[a * NB : a * NB + NB, cols] * mixed[a, :, cols].astype(F32)
                    + v[:, a * NB : a * NB + NB]
                )

    ex_e(0, 0, BL, 0, GW).recv()
    fine_terms(0)
    back_hidden(0)
    ex_e(1, 0, BL, GW, GW).recv()
    fine_terms(1)
    sf.start_a()
    back_hidden(1)

    def sums(i, total):
        a = i // 8
        at = pl.ds(pl.multiple_of((i % 8) * 16, 16), 16)
        v = tok[a, at, :].astype(F32)
        inv = lax.rsqrt(jnp.mean(v * v, axis=-1, keepdims=True) + EPS)
        prod = bhid[a, at, :] * (v * inv)
        return total + prod[:8] + prod[8:]

    gm = lax.fori_loop(0, BL * 8, sums, jnp.zeros((8, D), F32))
    gm = jnp.sum(gm, axis=0, keepdims=True)
    gl = jnp.sum(glm8[...], axis=0, keepdims=True)
    for d in range(G):
        gloc[d, 0:1, :] = gm[:, d * GW : (d + 1) * GW]
        gloc[d, 1:2, :] = gl[:, d * GW : (d + 1) * GW]
        gloc[d, 2:, :] = jnp.zeros((6, GW), F32)
    sf.start_gain()
    sf.start_b()
    weights_third()

    def last(i, carry):
        a = i // 8
        at = pl.ds(pl.multiple_of((i % 8) * 16, 16), 16)
        to = pl.ds(pl.multiple_of(i * 16, 16), 16)
        v = tok[a, at, :].astype(F32)
        inv = lax.rsqrt(jnp.mean(v * v, axis=-1, keepdims=True) + EPS)
        normed = v * inv
        w1 = bhid[a, at, :] * gain[...]
        center = jnp.mean(w1 * normed, axis=-1, keepdims=True)
        gin[a, at, :] = (bmi[to, :] + inv * (w1 - normed * center)).astype(BF16)
        return carry

    lax.fori_loop(0, BL * 8, last, 0)
    sf.start_c()
    sc.start_d()
    sf.start_d()
    recv_all(z_copy, NZ)
    v = zbuf[z].astype(F32)
    for k in range(NZ - 1):
        v = v + zrecv[k].astype(F32)
    wsum[...] = v

    sent_all(gz, NZ)
    for k in range(1, NX):
        for j in range(NY):
            ga_x(k, j).wait_send()
            gb_y(k, j).wait_send()
    for copy in (ga_y, gb_x, xa_copy, yb_copy, ya_copy, xb_copy):
        sent_all(copy, 4)
    for k in range(NX):
        ga_c(k).wait_send()
        gb_c(k).wait_send()
        core_copy(k).wait_send()
    sent_all(z_copy, NZ)
    for h in range(2):
        ex_a(h, 0, BL, GW * h, GW).sent()
        ex_b(h, 2 * h, 2, 0, QW).sent()
        ex_d(1 + h, 2, 2, GW * h, GW).sent()
        ex_e(h, 0, BL, GW * h, GW).sent()
    ex_d(0, 0, 2, 0, QW).sent()
    sc.finish()
    sf.finish()


def finish_kernel(
    gin, layer, wsum, fevery, cevery, gevery,
    ogin, olayer, ogu, odn, ofine, ocoarse, omix, omlp,
):
    olayer[0] = layer[...]
    ogin[0] = gin[0]

    @pl.when(pl.program_id(0) == 0)
    def _():
        scale = 1.0 / math.sqrt(8 * NC * NB)
        ogu[...] = wsum[:, : 2 * FF] * scale
        odn[...] = wsum[:, 2 * FF :] * scale
        lower = lax.broadcasted_iota(jnp.int32, (128, 128), 0) >= lax.broadcasted_iota(
            jnp.int32, (128, 128), 1
        )
        small = 1.0 / math.sqrt(8 * NC * GW)
        for d in range(G):
            ofine[d] = jnp.where(lower, fevery[d].astype(F32) * small, 0.0)
            ocoarse[d] = jnp.where(lower, cevery[d].astype(F32) * small, 0.0)
            omix[:, d * GW : (d + 1) * GW] = gevery[d, 4:5, :] * scale
            omlp[:, d * GW : (d + 1) * GW] = gevery[d, 5:6, :] * scale


def whole(*shape):
    return pl.BlockSpec(shape, lambda i: (0,) * len(shape))


def vmem(n):
    return [pl.BlockSpec(memory_space=pltpu.VMEM)] * n


def on_device(tokens, cotangent, gain_mix, gain_mlp, fine, coarse, w_gate_up, w_down):
    S = jax.ShapeDtypeStruct
    V = pltpu.VMEM
    parts = pl.pallas_call(
        layer_kernel,
        name="layer",
        out_shape=(
            S((BL, NB, D), BF16),
            S((ROWS, D), BF16),
            S((4, WC), F32),
            S((G, 128, 128), BF16),
            S((G, 128, 128), BF16),
            S((G, 8, 128), F32),
        ),
        in_specs=vmem(8),
        out_specs=tuple(vmem(6)),
        scratch_shapes=[
            V((BL, NB, D), BF16),
            V((BL, NB, D), BF16),
            V((NC, BW, QW), BF16),
            V((NC, BW, QW), BF16),
            V((BL, NB, D), BF16),
            V((BL, NB, D), BF16),
            V((NC, BW, QW), BF16),
            V((NC, BW, QW), BF16),
            V((BL, NB, D), BF16),
            V((BL, NB, D), F32),
            V((2, NC * BW, GW), F32),
            V((2, NC * BW, GW), F32),
            V((2, NC * BW, GW), F32),
            V((NZ, 4, WC), BF16),
            V((32, WC), F32),
            V((NX, 2, NY, 32, WC), BF16),
            V((ROWS, D), F32),
            V((ROWS, 128), F32),
            V((ROWS, D), BF16),
            V((ROWS, FF), BF16),
            V((ROWS, 2 * FF), BF16),
            V((ROWS, D), F32),
            V((8, D), F32),
            V((NX, 2, NY, 32, WC), BF16),
            V((NX, NY, 32, WC), BF16),
            V((3, NY, 32, WC // 2), BF16),
            V((3, NX, 32, WC // 2), BF16),
            V((NY, 32, WC // 2), F32),
            V((NX, 32, WC // 2), F32),
            V((NY, 32, WC // 2), BF16),
            V((NX, 32, WC // 2), BF16),
            V((3, 32, WC // 2), BF16),
            V((3, 32, WC // 2), BF16),
            V((8, 4, WC), BF16),
            V((7, 4, WC), BF16),
            dma(2), dma(2), dma(2), dma(2),
            dma(3), dma(3), dma(2), dma(2),
            dma(7, 8), dma(7, 8), dma(4, 4), dma(4, 4), dma(4, 4), dma(4, 4),
            dma(4), dma(4), dma(2, 4), dma(2, 4), dma(2, 4), dma(2, 4), dma(8), dma(8),
            V((8, 8, 128), F32), V((8, 8, 128), F32), dma(2), dma(2),
            *small_scratch(), *small_scratch(),
        ],
        compiler_params=pltpu.CompilerParams(
            collective_id=0, has_side_effects=True, vmem_limit_bytes=63 * 1024 * 1024
        ),
    )(
        tokens.reshape(BL, NB, D), cotangent.reshape(ROWS, D),
        gain_mix.reshape(1, D), gain_mlp.reshape(1, D), fine, coarse, w_gate_up, w_down,
    )
    gin, layer, ogu, odn, ofine, ocoarse, omix, omlp = pl.pallas_call(
        finish_kernel,
        name="finish",
        out_shape=(
            S((1, ROWS, D), BF16),
            S((1, ROWS, D), BF16),
            S((4, 2 * FF), F32),
            S((4, FF), F32),
            S((G, NB, NB), F32),
            S((G, NC, NC), F32),
            S((1, D), F32),
            S((1, D), F32),
        ),
        grid=(BL,),
        in_specs=[
            pl.BlockSpec((1, NB, D), lambda i: (i, 0, 0)),
            pl.BlockSpec((NB, D), lambda i: (i, 0)),
            whole(4, WC), whole(G, 128, 128), whole(G, 128, 128), whole(G, 8, 128),
        ],
        out_specs=(
            pl.BlockSpec((1, NB, D), lambda i: (0, i, 0)),
            pl.BlockSpec((1, NB, D), lambda i: (0, i, 0)),
            whole(4, 2 * FF), whole(4, FF), whole(G, NB, NB), whole(G, NC, NC),
            whole(1, D), whole(1, D),
        ),
    )(*parts)
    return (layer, gin, ogu, odn, ofine, ocoarse, omix.reshape(D), omlp.reshape(D))


def solution(mesh):
    rows = P("dp", "seq", None)
    weights = P(("dp", "seq"), None)
    return jax.shard_map(
        on_device,
        mesh=mesh,
        in_specs=(rows, rows, P(), P(), P(), P(), weights, weights),
        out_specs=(rows, rows, weights, weights, P(), P(), P(), P()),
        check_vma=False,
    )
```
